32 devices in a mesh: dp: 16 (over z, y, x), tensor: 2 (over core).
Axes of the slice: x: 2, y: 2, z: 4, core: 2. Of those that a mesh axis runs over, the one named last changes fastest.
Arguments:
- block_input: bfloat16 [4096, 1024], P(('dp', 'tensor')), may hold values from -32 to 32
- segments: int32 [16, 256], P('dp'), may hold values from 0 to 31, as said below
- positions: int32 [16, 256], P('dp'), may hold values from 0 to 2302, as said below
- norm1_gain: bfloat16 [1024], replicated, may hold values from 0.5 to 1.5
- w_query: bfloat16 [1024, 1024], P('dp', 'tensor'), may hold values from -0.1875 to 0.1875
- w_key: bfloat16 [1024, 512], P('dp', 'tensor'), may hold values from -0.1875 to 0.1875
- w_value: bfloat16 [1024, 512], P('dp', 'tensor'), may hold values from -0.1875 to 0.1875
- w_out: bfloat16 [1024, 1024], P('tensor', 'dp'), may hold values from -0.5 to 0.5
- query_gain: bfloat16 [64], replicated, may hold values from 0.5 to 2
- key_gain: bfloat16 [64], replicated, may hold values from 0.5 to 2
- norm2_gain: bfloat16 [1024], replicated, may hold values from 0.5 to 1.5
- w_gate: bfloat16 [1024, 4608], P('dp', 'tensor'), may hold values from -0.1875 to 0.1875
- w_up: bfloat16 [1024, 4608], P('dp', 'tensor'), may hold values from -0.1875 to 0.1875
- w_down: bfloat16 [4608, 1024], P('tensor', 'dp'), may hold values from -0.1875 to 0.1875
- grad_out: bfloat16 [4096, 1024], P(('dp', 'tensor')), may hold values from -6 to 6
Outputs:
- block_out: bfloat16 [4096, 1024], P(('dp', 'tensor'))
- grad_input: float32 [4096, 1024], P(('dp', 'tensor'))
- grad_norm1_gain: float32 [1024], replicated
- grad_w_query: float32 [1024, 1024], P('dp', 'tensor')
- grad_w_key: float32 [1024, 512], P('dp', 'tensor')
- grad_w_value: float32 [1024, 512], P('dp', 'tensor')
- grad_w_out: float32 [1024, 1024], P('tensor', 'dp')
- grad_query_gain: float32 [64], replicated
- grad_key_gain: float32 [64], replicated
- grad_norm2_gain: float32 [1024], replicated
- grad_w_gate: float32 [1024, 4608], P('dp', 'tensor')
- grad_w_up: float32 [1024, 4608], P('dp', 'tensor')
- grad_w_down: float32 [4608, 1024], P('tensor', 'dp')
The draws below stay inside these ranges and needn't reach their ends.
Inputs may be any that keep to these rules, and one draw needn't show every extreme that they name: `segments`: in every sequence of 256 tokens the segment numbers start at 0 and never fall; each number is one document, and documents begin only at token indices that are multiples of 8. Within a document positions rise by one from token to token; every document but a sequence's first starts at position 0.
All inputs are finite; a program needn't handle non-finite values.
Results may differ from the reference program's by a relative error of at most 0.013.
The reference program's roundings to bfloat16 on the way count: a program that leaves them out, or rounds other values in their place, can miss the bound.
Values may be sent and summed in bfloat16 or wider, within the bound.
No kernel may reach another device: no remote copies, remote signals or barrier semaphores. Data moves between devices by JAX's collectives and lax.ppermute only.
A program may use at most 128 MiB of HBM per device.

```python
import math
import jax
import jax.numpy as jnp
from jax import lax

D = 1024
H = 16
KV = 8
HD = 64
FF = 4608
LEN = 256
SEQS = 16
TOKENS = 4096


def document_layout(key):
    layout_key = jax.random.fold_in(key, 11)
    mark_key, offset_key = jax.random.split(layout_key)
    index_grid = jnp.broadcast_to(jnp.arange(LEN, dtype=jnp.int32)[None, :], (SEQS, LEN))
    on_grid = index_grid % 8 == 0
    marks = jax.random.randint(mark_key, (SEQS, LEN), 0, max(LEN * 5 // 64, 2))
    starts = jnp.where((marks == 0) & on_grid, 1, 0).astype(jnp.int32)
    starts = starts.at[0, :].set(0)
    starts = starts.at[SEQS - 1, :].set(on_grid[0].astype(jnp.int32))
    starts = starts.at[:, 0].set(1)
    segment_ids = jnp.cumsum(starts, axis=1) - 1
    first_index = lax.cummax(starts * index_grid, axis=1)
    offsets = jax.random.randint(offset_key, (SEQS, 1), 0, 2048)
    offsets = offsets.at[0, 0].set(2047)
    position_ids = index_grid - first_index + jnp.where(segment_ids == 0, offsets, 0)
    return (segment_ids.astype(jnp.int32), position_ids.astype(jnp.int32))


def draw_segments(key, part):
    return document_layout(key)[0]


def draw_positions(key, part):
    return document_layout(key)[1]


def draw_block_input(key, part):
    row_key, col_key, base_key = jax.random.split(jax.random.fold_in(key, 31), 3)
    row_scale = jnp.exp(jax.random.uniform(row_key, (TOKENS, 1), minval=math.log(0.4), maxval=math.log(4.0)))
    col_scale = jnp.exp(jax.random.uniform(col_key, (1, D), minval=math.log(0.5), maxval=math.log(2.0)))
    base = jnp.clip(jax.random.normal(base_key, (TOKENS, D)), -4.0, 4.0)
    return (base * row_scale * col_scale).astype(jnp.bfloat16)


def draw_query_gain(key, part):
    gain_key = jax.random.fold_in(key, 41)
    values = jax.random.uniform(gain_key, (HD,), minval=0.5, maxval=2.0)
    return values.astype(jnp.bfloat16)


def draw_key_gain(key, part):
    gain_key = jax.random.fold_in(key, 43)
    values = jax.random.uniform(gain_key, (HD,), minval=0.5, maxval=2.0)
    return values.astype(jnp.bfloat16)


def spiked(array, rng, source, target, parts, factor):
    owner, partner = [(jnp.arange(array.shape[position]) // (array.shape[position] // parts)).reshape([-1 if axis == position else 1 for axis in range(array.ndim)]) for position in (source, target)]
    chosen = jax.random.permutation(rng, parts)[partner]
    strong = (owner == chosen) | (owner == (partner + parts // 2) % parts)
    return jnp.where(strong, factor * array, array)


def levels(own_key, extent, cuts, low, high):
    factor_of, own = 1.0, jax.random.fold_in(own_key, 6)
    for dim, parts in cuts:
        steps = jnp.exp(jax.random.uniform(jax.random.fold_in(own, dim), (parts,), jnp.float32, low / len(cuts), high / len(cuts)))
        factor_of = factor_of * jnp.repeat(steps, extent[dim] // parts).reshape([-1 if axis == dim else 1 for axis in range(len(extent))])
    return factor_of


def noise(stream_key, dims, deviation, reach, pieces=(), kind=jnp.bfloat16):
    values = jax.random.normal(stream_key, dims, jnp.float32) * deviation
    if len(pieces) > 0:
        values = levels(stream_key, dims, pieces, -0.22, 0.18) * values
    return jnp.clip(values, min=-reach, max=reach).astype(kind)


def noise_with(own_key, shape, deviation, limit, shards, heavy, held_as=jnp.bfloat16):
    values = deviation * jax.random.normal(own_key, shape, jnp.float32)
    if shards:
        values = values * levels(own_key, shape, shards, -0.22, 0.18)
    return jnp.clip(spiked(values, jax.random.fold_in(own_key, 3), *heavy), -limit, limit).astype(held_as)


def setup_inputs(seed: int = 0) -> dict:
    key_of = jax.random.split(jax.random.key(seed), 16)
    return {
        "block_input": draw_block_input(jax.random.fold_in(key_of[15], 71), 0),
        "segments": draw_segments(jax.random.fold_in(key_of[15], 71), 0),
        "positions": draw_positions(jax.random.fold_in(key_of[15], 71), 0),
        "norm1_gain": jnp.clip(1.0 + 0.1 * jax.random.normal(key_of[3], (D,), jnp.float32), 0.5, 1.5).astype(jnp.bfloat16),
        "w_query": noise(key_of[4], (D, H * HD), D ** -0.5, 0.1875, ((0, 16), (1, 2))),
        "w_key": noise(key_of[5], (D, KV * HD), D ** -0.5, 0.1875, ((0, 16), (1, 2))),
        "w_value": noise(key_of[6], (D, KV * HD), D ** -0.5, 0.1875, ((0, 16), (1, 2))),
        "w_out": noise(key_of[7], (H * HD, D), (H * HD // 8) ** -0.5, 0.5, ((0, 2), (1, 16))),
        "query_gain": draw_query_gain(jax.random.fold_in(key_of[15], 71), 0),
        "key_gain": draw_key_gain(jax.random.fold_in(key_of[15], 71), 0),
        "norm2_gain": jnp.clip(1.0 + 0.1 * jax.random.normal(key_of[10], (D,), jnp.float32), 0.5, 1.5).astype(jnp.bfloat16),
        "w_gate": noise(key_of[11], (D, FF), D ** -0.5, 0.1875, ((0, 16), (1, 2))),
        "w_up": noise(key_of[12], (D, FF), D ** -0.5, 0.1875, ((0, 16), (1, 2))),
        "w_down": noise(key_of[13], (FF, D), (FF // 4) ** -0.5, 0.1875, ((0, 2), (1, 16))),
        "grad_out": noise_with(key_of[14], (TOKENS, D), 1.0, 6.0, ((0, 32),), (0, 1, 32, 2.75)),
    }


epsilon = 1e-05
rope_base = 1000000.0
masked_score = -1e+30

def inverse_rms(values):
    return lax.rsqrt(lax.optimization_barrier(jnp.mean(values * values, axis=-1, keepdims=True)) + epsilon)

def rope_tables(positions, head_width):
    half_width = head_width // 2
    freq_index = jnp.arange(half_width).astype(jnp.float32)
    frequency = rope_base ** (-(2.0 * freq_index) / head_width)
    angles = positions.astype(jnp.float32)[:, None] * frequency[None, :]
    return (jnp.cos(angles), jnp.sin(angles))

def rotate(values, cosine, sine_table):
    half_width = values.shape[-1] // 2
    first_half = values[..., :half_width]
    second_half = values[..., half_width:]
    cosine_rows = cosine[:, None, :]
    sine_rows = sine_table[:, None, :]
    return jnp.concatenate([first_half * cosine_rows - second_half * sine_rows, second_half * cosine_rows + first_half * sine_rows], axis=-1)

def rotate_back(grads, cosine, sine_table):
    half_width = grads.shape[-1] // 2
    first_half = grads[..., :half_width]
    second_half = grads[..., half_width:]
    cosine_rows = cosine[:, None, :]
    sine_rows = sine_table[:, None, :]
    return jnp.concatenate([first_half * cosine_rows + second_half * sine_rows, second_half * cosine_rows - first_half * sine_rows], axis=-1)

def allowed_pairs(segment_row):
    length = segment_row.shape[0]
    row_index = lax.broadcasted_iota(jnp.int32, (length, length), 0)
    col_index = lax.broadcasted_iota(jnp.int32, (length, length), 1)
    return (col_index <= row_index) & (segment_row[:, None] == segment_row[None, :])

def head_norm(projected, gain_row):
    inverse_scale = inverse_rms(projected)
    unit_rows = projected * inverse_scale
    return (unit_rows, inverse_scale, unit_rows * gain_row[None, None, :])

def head_norm_back(grad_normed, unit_rows, inverse_scale, gain_row):
    gain_part = lax.optimization_barrier(jnp.sum(unit_rows * grad_normed, axis=(0, 1)))
    weighted = grad_normed * gain_row[None, None, :]
    grad_proj = inverse_scale * (weighted - unit_rows * lax.optimization_barrier(jnp.mean(weighted * unit_rows, axis=-1, keepdims=True)))
    return (grad_proj, gain_part)

def group_scores(query_group, key_group, allowed, score_scale):
    scores = jnp.einsum('igd,jd->gij', query_group.astype(jnp.float32), key_group.astype(jnp.float32)) * score_scale
    return jnp.where(allowed[None, :, :], scores, masked_score)

def group_forward(query_group, key_group, value_group, allowed, score_scale):
    scores = group_scores(query_group, key_group, allowed, score_scale)
    row_max = lax.optimization_barrier(jnp.max(scores, axis=-1, keepdims=True))
    log_total = row_max + jnp.log(lax.optimization_barrier(jnp.sum(jnp.exp(scores - row_max), axis=-1, keepdims=True)))
    low_weights = jnp.exp(scores - log_total).astype(jnp.bfloat16)
    attended = jnp.einsum('gij,jd->igd', low_weights.astype(jnp.float32), value_group.astype(jnp.float32))
    return (attended.astype(jnp.bfloat16), log_total[..., 0])

def group_backward(query_group, key_group, value_group, grad_group, log_total, allowed, score_scale):
    scores = group_scores(query_group, key_group, allowed, score_scale)
    low_weights = jnp.exp(scores - log_total[..., None]).astype(jnp.bfloat16)
    wide_weights = low_weights.astype(jnp.float32)
    grad_wide = grad_group.astype(jnp.float32)
    grad_weights = jnp.einsum('igd,jd->gij', grad_wide, value_group.astype(jnp.float32))
    row_delta = lax.optimization_barrier(jnp.sum(wide_weights * grad_weights, axis=-1, keepdims=True))
    grad_scores = (wide_weights * (grad_weights - row_delta) * score_scale).astype(jnp.bfloat16)
    grad_scores = grad_scores.astype(jnp.float32)
    grad_query = jnp.einsum('gij,jd->igd', grad_scores, key_group.astype(jnp.float32))
    grad_key = jnp.einsum('gij,igd->jd', grad_scores, query_group.astype(jnp.float32))
    grad_value = jnp.einsum('gij,igd->jd', wide_weights, grad_wide).astype(jnp.bfloat16)
    return (grad_query, grad_key, grad_value)

def attention_forward(query_rot, key_rot, value_proj, allowed):
    length, query_heads, head_width = query_rot.shape
    shared_heads = key_rot.shape[1]
    group_size = query_heads // shared_heads
    score_scale = head_width ** (-0.5)
    query_groups = jnp.moveaxis(query_rot.reshape(length, shared_heads, group_size, head_width), 1, 0)
    key_groups = jnp.moveaxis(key_rot, 1, 0)
    value_groups = jnp.moveaxis(value_proj, 1, 0)
    attended, log_total = lax.map(lambda members: group_forward(members[0], members[1], members[2], allowed, score_scale), (query_groups, key_groups, value_groups))
    attended = jnp.moveaxis(attended, 0, 1).reshape(length, query_heads * head_width)
    return (attended, log_total, (query_groups, key_groups, value_groups))

def attention_backward(groups, grad_attended, log_total, allowed):
    query_groups, key_groups, value_groups = groups
    shared_heads, length, group_size, head_width = query_groups.shape
    score_scale = head_width ** (-0.5)
    grad_groups = jnp.moveaxis(grad_attended.reshape(length, shared_heads, group_size, head_width), 1, 0)
    grad_query, grad_key, grad_value = lax.map(lambda members: group_backward(members[0], members[1], members[2], members[3], members[4], allowed, score_scale), (query_groups, key_groups, value_groups, grad_groups, log_total))
    grad_query = jnp.moveaxis(grad_query, 0, 1).reshape(length, shared_heads * group_size, head_width)
    grad_key = jnp.moveaxis(grad_key, 0, 1)
    grad_value = jnp.moveaxis(grad_value, 0, 1).reshape(length, shared_heads * head_width)
    return (grad_query, grad_key, grad_value)

def sequence_pass(seq_input, seq_grad, seq_segments, seq_positions, params):
    norm1_gain, w_query, w_key, w_value, w_out, query_gain, key_gain, norm2_gain, w_gate, w_up, w_down = params
    gain_one = norm1_gain.astype(jnp.float32)
    gain_two = norm2_gain.astype(jnp.float32)
    gain_query = query_gain.astype(jnp.float32)
    gain_key = key_gain.astype(jnp.float32)
    own_input = seq_input.astype(jnp.float32)
    length = own_input.shape[0]
    scale_one = inverse_rms(own_input)
    unit_one = own_input * scale_one
    normed_one = (unit_one * gain_one).astype(jnp.bfloat16)
    query_proj = jnp.dot(normed_one, w_query, preferred_element_type=jnp.float32).reshape(length, -1, HD)
    key_proj = jnp.dot(normed_one, w_key, preferred_element_type=jnp.float32).reshape(length, -1, HD)
    value_proj = jnp.dot(normed_one, w_value, preferred_element_type=jnp.float32).astype(jnp.bfloat16).reshape(length, -1, HD)
    query_unit, query_scale, query_normed = head_norm(query_proj, gain_query)
    key_unit, key_scale, key_normed = head_norm(key_proj, gain_key)
    cosine, sine_table = rope_tables(seq_positions, HD)
    query_rot = rotate(query_normed, cosine, sine_table).astype(jnp.bfloat16)
    key_rot = rotate(key_normed, cosine, sine_table).astype(jnp.bfloat16)
    allowed = allowed_pairs(seq_segments)
    attended, log_total, groups = attention_forward(query_rot, key_rot, value_proj, allowed)
    hidden = own_input + jnp.dot(attended, w_out, preferred_element_type=jnp.float32)
    scale_two = inverse_rms(hidden)
    unit_two = hidden * scale_two
    normed_two = (unit_two * gain_two).astype(jnp.bfloat16)
    gate_proj = jnp.dot(normed_two, w_gate, preferred_element_type=jnp.float32)
    up_proj = jnp.dot(normed_two, w_up, preferred_element_type=jnp.float32)
    sigmoid_gate = jax.nn.sigmoid(gate_proj)
    silu_gate = gate_proj * sigmoid_gate
    activated = (silu_gate * up_proj).astype(jnp.bfloat16)
    block_out = (hidden + jnp.dot(activated, w_down, preferred_element_type=jnp.float32)).astype(jnp.bfloat16)
    grad_act = jnp.dot(seq_grad, w_down.T, preferred_element_type=jnp.float32)
    grad_w_down = jnp.dot(activated.T, seq_grad, preferred_element_type=jnp.float32)
    grad_gate = (grad_act * up_proj * sigmoid_gate * (1.0 + gate_proj * (1.0 - sigmoid_gate))).astype(jnp.bfloat16)
    grad_up = (grad_act * silu_gate).astype(jnp.bfloat16)
    grad_w_gate = jnp.dot(normed_two.T, grad_gate, preferred_element_type=jnp.float32)
    grad_w_up = jnp.dot(normed_two.T, grad_up, preferred_element_type=jnp.float32)
    grad_normed_two = jnp.dot(grad_gate, w_gate.T, preferred_element_type=jnp.float32) + jnp.dot(grad_up, w_up.T, preferred_element_type=jnp.float32)
    gain_two_part = lax.optimization_barrier(jnp.sum(unit_two * grad_normed_two, axis=0))
    weighted_two = grad_normed_two * gain_two
    grad_hidden = seq_grad.astype(jnp.float32) + scale_two * (weighted_two - unit_two * lax.optimization_barrier(jnp.mean(weighted_two * unit_two, axis=-1, keepdims=True)))
    grad_branch = grad_hidden.astype(jnp.bfloat16)
    grad_attended = jnp.dot(grad_branch, w_out.T, preferred_element_type=jnp.float32).astype(jnp.bfloat16)
    grad_w_out = jnp.dot(attended.T, grad_branch, preferred_element_type=jnp.float32)
    grad_query_rot, grad_key_rot, grad_value = attention_backward(groups, grad_attended, log_total, allowed)
    grad_query_normed = rotate_back(grad_query_rot, cosine, sine_table)
    grad_key_normed = rotate_back(grad_key_rot, cosine, sine_table)
    grad_query_proj, query_gain_part = head_norm_back(grad_query_normed, query_unit, query_scale, gain_query)
    grad_key_proj, key_gain_part = head_norm_back(grad_key_normed, key_unit, key_scale, gain_key)
    grad_query_proj = grad_query_proj.astype(jnp.bfloat16).reshape(length, -1)
    grad_key_proj = grad_key_proj.astype(jnp.bfloat16).reshape(length, -1)
    grad_w_query = jnp.dot(normed_one.T, grad_query_proj, preferred_element_type=jnp.float32)
    grad_w_key = jnp.dot(normed_one.T, grad_key_proj, preferred_element_type=jnp.float32)
    grad_w_value = jnp.dot(normed_one.T, grad_value, preferred_element_type=jnp.float32)
    grad_normed_one = jnp.dot(grad_query_proj, w_query.T, preferred_element_type=jnp.float32) + jnp.dot(grad_key_proj, w_key.T, preferred_element_type=jnp.float32) + jnp.dot(grad_value, w_value.T, preferred_element_type=jnp.float32)
    gain_one_part = lax.optimization_barrier(jnp.sum(unit_one * grad_normed_one, axis=0))
    weighted_one = grad_normed_one * gain_one
    grad_input = grad_hidden + scale_one * (weighted_one - unit_one * lax.optimization_barrier(jnp.mean(weighted_one * unit_one, axis=-1, keepdims=True)))
    grads = (gain_one_part, grad_w_query, grad_w_key, grad_w_value, grad_w_out, query_gain_part, key_gain_part, gain_two_part, grad_w_gate, grad_w_up, grad_w_down)
    return (block_out, grad_input, grads)

def reference(block_input, segments, positions, norm1_gain, w_query, w_key, w_value, w_out, query_gain, key_gain, norm2_gain, w_gate, w_up, w_down, grad_out):
    params = (norm1_gain, w_query, w_key, w_value, w_out, query_gain, key_gain, norm2_gain, w_gate, w_up, w_down)
    inputs_seq = block_input.reshape(SEQS, LEN, D)
    grads_seq = grad_out.reshape(SEQS, LEN, D)
    starting = (jnp.zeros((D,), jnp.float32), jnp.zeros(w_query.shape, jnp.float32), jnp.zeros(w_key.shape, jnp.float32), jnp.zeros(w_value.shape, jnp.float32), jnp.zeros(w_out.shape, jnp.float32), jnp.zeros((HD,), jnp.float32), jnp.zeros((HD,), jnp.float32), jnp.zeros((D,), jnp.float32), jnp.zeros(w_gate.shape, jnp.float32), jnp.zeros(w_up.shape, jnp.float32), jnp.zeros(w_down.shape, jnp.float32))

    def one_sequence(running_sums, members):
        seq_out, seq_grad_in, grads = sequence_pass(members[0], members[1], members[2], members[3], params)
        running_sums = jax.tree.map(lambda running, addend: running + addend, running_sums, grads)
        return (running_sums, (seq_out, seq_grad_in))
    totals, (outputs, grad_inputs) = lax.scan(one_sequence, starting, (inputs_seq, grads_seq, segments, positions))
    return (outputs.reshape(TOKENS, D), grad_inputs.reshape(TOKENS, D), totals[0], totals[1], totals[2], totals[3], totals[4], totals[5], totals[6], totals[7], totals[8], totals[9], totals[10])
```

```python
import jax
import jax.numpy as jnp
from jax import lax
from jax.experimental import pallas as pl
from jax.experimental.pallas import tpu as pltpu
from jax.sharding import PartitionSpec as P

HD = 64
PLANE = 4

epsilon = 1e-05
rope_base = 1000000.0
masked_score = -1e30

f32 = jnp.float32
bf16 = jnp.bfloat16


def inverse_rms(values):
    return lax.rsqrt(jnp.mean(values * values, axis=-1, keepdims=True) + epsilon)


def dot_nn(a, b):
    return lax.dot_general(a, b, (((1,), (0,)), ((), ())), preferred_element_type=f32)


def dot_nt(a, b):
    return lax.dot_general(a, b, (((1,), (1,)), ((), ())), preferred_element_type=f32)


def dot_tn(a, b):
    return lax.dot_general(a, b, (((0,), (0,)), ((), ())), preferred_element_type=f32)


def swap_halves(values):
    half = values.shape[-1] // 2
    return jnp.concatenate([values[:, half:], values[:, :half]], axis=-1)


def rope_tables(positions, head_width):
    half_width = head_width // 2
    freq_index = jnp.arange(half_width).astype(f32)
    frequency = rope_base ** (-(2.0 * freq_index) / head_width)
    angles = positions.astype(f32)[..., None] * frequency
    cosine, sine = jnp.cos(angles), jnp.sin(angles)
    return (
        jnp.concatenate([cosine, cosine], axis=-1),
        jnp.concatenate([-sine, sine], axis=-1),
    )


def attention_forward_kernel(
    qkv_ref, cos_ref, sin_ref, seg_col_ref, seg_row_ref, gain_ref, o_ref, p_ref
):
    length = cos_ref.shape[1]
    qkv = qkv_ref[...].reshape(length, qkv_ref.shape[-1])
    cosine, sine = cos_ref[0], sin_ref[0]
    row = lax.broadcasted_iota(jnp.int32, (length, length), 0)
    col = lax.broadcasted_iota(jnp.int32, (length, length), 1)
    allowed = (col <= row) & (seg_col_ref[0] == seg_row_ref[0])

    def rotated(lo, gain):
        raw = qkv[:, lo : lo + HD]
        normed = raw * inverse_rms(raw) * gain
        return (normed * cosine + swap_halves(normed) * sine).astype(bf16)

    key = rotated(2 * HD, gain_ref[1:2, :])
    value = qkv[:, 3 * HD : 4 * HD].astype(bf16)
    outs = []
    for head in range(2):
        query = rotated(head * HD, gain_ref[0:1, :])
        scores = jnp.where(allowed, dot_nt(query, key) * HD**-0.5, masked_score)
        row_max = jnp.max(scores, axis=-1, keepdims=True)
        total = jnp.sum(jnp.exp(scores - row_max), axis=-1, keepdims=True)
        weights = jnp.exp(scores - (row_max + jnp.log(total))).astype(bf16)
        p_ref[0, head] = weights
        outs.append(dot_nn(weights, value).astype(bf16))
    o_ref[...] = jnp.concatenate(outs, axis=-1).reshape(o_ref.shape)


def attention_backward_kernel(
    qkv_ref, cos_ref, sin_ref, gain_ref, p_ref, do_ref, dqkv_ref, dgain_ref
):
    length = cos_ref.shape[1]
    qkv = qkv_ref[...].reshape(length, qkv_ref.shape[-1])
    cosine, sine = cos_ref[0], sin_ref[0]
    grad_o = do_ref[...].reshape(length, 2 * HD)

    def forward(lo, gain):
        raw = qkv[:, lo : lo + HD]
        scale = inverse_rms(raw)
        unit = raw * scale
        normed = unit * gain
        return unit, scale, (normed * cosine + swap_halves(normed) * sine).astype(bf16)

    def backward(grad_rot, unit, scale, gain):
        grad_normed = grad_rot * cosine - swap_halves(grad_rot) * sine
        gain_part = jnp.sum(unit * grad_normed, axis=0, keepdims=True)
        weighted = grad_normed * gain
        mean = jnp.mean(weighted * unit, axis=-1, keepdims=True)
        return (scale * (weighted - unit * mean)).astype(bf16), gain_part

    query_gain, key_gain = gain_ref[0:1, :], gain_ref[1:2, :]
    key_unit, key_scale, key = forward(2 * HD, key_gain)
    value = qkv[:, 3 * HD : 4 * HD].astype(bf16)
    grad_key = jnp.zeros((length, HD), f32)
    grad_value = jnp.zeros((length, HD), f32)
    query_gain_part = jnp.zeros((1, HD), f32)
    parts = []
    for head in range(2):
        query_unit, query_scale, query = forward(head * HD, query_gain)
        low = p_ref[0, head]
        wide = low.astype(f32)
        grad_head = grad_o[:, head * HD : (head + 1) * HD]
        grad_weights = dot_nt(grad_head, value)
        delta = jnp.sum(wide * grad_weights, axis=-1, keepdims=True)
        grad_scores = (wide * (grad_weights - delta) * HD**-0.5).astype(bf16)
        grad_value += dot_tn(low, grad_head)
        grad_key += dot_tn(grad_scores, query)
        part, gain_part = backward(dot_nn(grad_scores, key), query_unit, query_scale, query_gain)
        query_gain_part += gain_part
        parts.append(part)
    part, key_gain_part = backward(grad_key, key_unit, key_scale, key_gain)
    parts += [part, grad_value.astype(bf16)]
    dqkv_ref[...] = jnp.concatenate(parts, axis=-1).reshape(dqkv_ref.shape)
    dgain_ref[0] = jnp.concatenate([query_gain_part, key_gain_part], axis=-1)


def token_block(seq_rows, width):
    return pl.BlockSpec((2, 1, seq_rows, width), lambda s: (0, s, 0, 0))


def seq_block(shape):
    return pl.BlockSpec((1,) + shape, lambda s: (s,) + (0,) * len(shape))


def attention_forward(qkv, cosine, sine, seg_col, seg_row, gains):
    _, seqs, half, width = qkv.shape
    length = 2 * half
    return pl.pallas_call(
        attention_forward_kernel,
        grid=(seqs,),
        in_specs=[
            token_block(half, width),
            seq_block((length, HD)),
            seq_block((length, HD)),
            seq_block((length, 1)),
            seq_block((1, length)),
            pl.BlockSpec((2, HD), lambda s: (0, 0)),
        ],
        out_specs=[token_block(half, 2 * HD), seq_block((2, length, length))],
        out_shape=[
            jax.ShapeDtypeStruct((2, seqs, half, 2 * HD), bf16),
            jax.ShapeDtypeStruct((seqs, 2, length, length), bf16),
        ],
        name="attention_forward",
    )(qkv, cosine, sine, seg_col, seg_row, gains)


def attention_backward(qkv, cosine, sine, gains, weights, grad_o):
    _, seqs, half, width = qkv.shape
    length = 2 * half
    return pl.pallas_call(
        attention_backward_kernel,
        grid=(seqs,),
        in_specs=[
            token_block(half, width),
            seq_block((length, HD)),
            seq_block((length, HD)),
            pl.BlockSpec((2, HD), lambda s: (0, 0)),
            seq_block((2, length, length)),
            token_block(half, 2 * HD),
        ],
        out_specs=[token_block(half, width), seq_block((1, 2 * HD))],
        out_shape=[
            jax.ShapeDtypeStruct((2, seqs, half, width), bf16),
            jax.ShapeDtypeStruct((seqs, 1, 2 * HD), f32),
        ],
        name="attention_backward",
    )(qkv, cosine, sine, gains, weights, grad_o)


def unxor(blocks, index):
    step = 1
    while step < len(blocks):
        odd = (index & step) != 0
        blocks = [
            jnp.where(odd, blocks[k ^ step], blocks[k]) for k in range(len(blocks))
        ]
        step *= 2
    return blocks


def pick(stacked, index):
    return lax.dynamic_index_in_dim(stacked, index, 0, keepdims=False)


def solution(mesh):
    devices = mesh.shape["dp"]
    depth = devices // PLANE

    def dp_swap(value, mask):
        return lax.ppermute(value, "dp", [(i, i ^ mask) for i in range(devices)])

    def core_swap(value):
        return lax.ppermute(value, "tensor", [(0, 1), (1, 0)])

    def body(
        block_input,
        segments,
        positions,
        norm1_gain,
        w_query,
        w_key,
        w_value,
        w_out,
        query_gain,
        key_gain,
        norm2_gain,
        w_gate,
        w_up,
        w_down,
        grad_out,
    ):
        me = lax.axis_index("dp")
        core = lax.axis_index("tensor")
        place, level = me % PLANE, me // PLANE
        half, width = block_input.shape
        rows = w_query.shape[0]

        def quarters(*arrays):
            parts = [jnp.moveaxis(a.reshape(rows, PLANE, -1), 1, 0) for a in arrays]
            return jnp.concatenate(parts, axis=-1)

        def plane_exchange(stacked):
            received = [pick(stacked, place)]
            for k in range(1, PLANE):
                received.append(dp_swap(pick(stacked, place ^ k), k))
            return jnp.stack(unxor(received, place))

        def gather_weights(stacked):
            mine = plane_exchange(stacked).reshape(PLANE * rows, -1)
            received = [mine] + [dp_swap(mine, k * PLANE) for k in range(1, depth)]
            return jnp.concatenate(unxor(received, level), axis=0)

        def scatter_grads(grad):
            stacked = grad.reshape(depth, PLANE * rows, -1)
            total = pick(stacked, level).astype(f32)
            for k in range(1, depth):
                total += dp_swap(pick(stacked, level ^ k), k * PLANE).astype(f32)
            summed = total.astype(bf16).reshape(PLANE, rows, -1)
            return jnp.moveaxis(plane_exchange(summed), 0, 1).astype(f32)

        def gather_tokens(block):
            chips = [block] + [dp_swap(block, k) for k in range(1, PLANE)]
            return lax.all_gather(jnp.concatenate(chips, axis=0), "tensor", axis=0)

        def reduce_tokens(partial_of):
            received = core_swap(partial_of(1 - core).astype(bf16))
            mine = (partial_of(core) + received.astype(f32)).reshape(PLANE, half, width)
            total = mine[0]
            for k in range(1, PLANE):
                total += dp_swap(mine[k].astype(bf16), k).astype(f32)
            return total

        gain_one = norm1_gain.astype(f32)
        gain_two = norm2_gain.astype(f32)
        head_gains = jnp.stack([query_gain, key_gain]).astype(f32)

        all_input = gather_tokens(block_input)
        attn_weights = gather_weights(quarters(w_query, w_key, w_value, w_out.T))
        layout = jnp.concatenate([segments, positions], axis=0)
        layout = jnp.stack([layout] + [dp_swap(layout, k) for k in range(1, PLANE)])
        ffn_weights = gather_weights(quarters(w_gate, w_up, w_down.T))
        grad_rows = gather_tokens(grad_out)

        w_qkv, w_out_t = attn_weights[:, : 4 * HD], attn_weights[:, 4 * HD :]
        units = w_gate.shape[1] // PLANE
        w_gu, w_down_t = ffn_weights[:, : 2 * units], ffn_weights[:, 2 * units :]
        tokens = 2 * PLANE * half

        wide_input = all_input.astype(f32)
        all_unit = wide_input * inverse_rms(wide_input)
        normed_one = (all_unit * gain_one).astype(bf16).reshape(tokens, width)
        qkv = dot_nn(normed_one, w_qkv).reshape(2, PLANE, half, 4 * HD)
        cosine, sine = rope_tables(layout[:, 1], HD)
        seg_row = layout[:, 0:1]
        seg_col = layout[:, 0, :, None]
        attended, weights = attention_forward(qkv, cosine, sine, seg_col, seg_row, head_gains)
        attended = attended.reshape(2, PLANE * half, 2 * HD)

        own_input = block_input.astype(f32)
        scale_one = inverse_rms(own_input)
        unit_one = own_input * scale_one
        hidden = own_input + reduce_tokens(lambda c: dot_nt(pick(attended, c), w_out_t))
        scale_two = inverse_rms(hidden)
        unit_two = hidden * scale_two
        normed_two = gather_tokens((unit_two * gain_two).astype(bf16)).reshape(tokens, width)

        grad_rows = grad_rows.reshape(tokens, width)
        grad_act = dot_nn(grad_rows, w_down_t)
        gate_up = dot_nn(normed_two, w_gu)
        gate_proj, up_proj = gate_up[:, :units], gate_up[:, units:]
        sigmoid_gate = jax.nn.sigmoid(gate_proj)
        silu_gate = gate_proj * sigmoid_gate
        activated = (silu_gate * up_proj).astype(bf16)
        grad_gate = (
            grad_act * up_proj * sigmoid_gate * (1.0 + gate_proj * (1.0 - sigmoid_gate))
        ).astype(bf16)
        grad_up = (grad_act * silu_gate).astype(bf16)
        grad_gu = jnp.concatenate([grad_gate, grad_up], axis=-1)
        grad_gu_halves = grad_gu.reshape(2, PLANE * half, 2 * units)
        grad_normed_two = reduce_tokens(lambda c: dot_nt(pick(grad_gu_halves, c), w_gu))

        gain_two_part = jnp.sum(unit_two * grad_normed_two, axis=0)
        weighted_two = grad_normed_two * gain_two
        grad_hidden = grad_out.astype(f32) + scale_two * (
            weighted_two - unit_two * jnp.mean(weighted_two * unit_two, axis=-1, keepdims=True)
        )
        grad_branch = gather_tokens(grad_hidden.astype(bf16)).reshape(tokens, width)

        ffn_grads = jnp.concatenate(
            [dot_tn(normed_two, grad_gu), dot_tn(grad_rows, activated)], axis=-1
        ).astype(bf16)
        ffn_grads = scatter_grads(ffn_grads)
        activated_halves = activated.reshape(2, PLANE * half, units)
        ffn_own = reduce_tokens(lambda c: dot_nt(pick(activated_halves, c), w_down_t))
        block_out = (hidden + ffn_own).astype(bf16)

        grad_attended = dot_nn(grad_branch, w_out_t).astype(bf16)
        grad_qkv, head_gain_parts = attention_backward(
            qkv, cosine, sine, head_gains, weights, grad_attended.reshape(2, PLANE, half, 2 * HD)
        )
        grad_qkv_halves = grad_qkv.reshape(2, PLANE * half, 4 * HD)
        grad_qkv = grad_qkv.reshape(tokens, 4 * HD)
        grad_normed_one = reduce_tokens(lambda c: dot_nt(pick(grad_qkv_halves, c), w_qkv))
        attended = attended.reshape(tokens, 2 * HD)
        attn_grads = jnp.concatenate(
            [dot_tn(normed_one, grad_qkv), dot_tn(grad_branch, attended)], axis=-1
        ).astype(bf16)
        attn_grads = scatter_grads(attn_grads)

        gain_one_part = jnp.sum(
            all_unit.reshape(tokens, width) * dot_nt(grad_qkv, w_qkv), axis=0
        )
        gain_parts = jnp.concatenate(
            [gain_one_part, gain_two_part, jnp.sum(head_gain_parts, axis=(0, 1))]
        ).reshape(-1, 128)
        spread = jnp.broadcast_to(gain_parts, (devices,) + gain_parts.shape)
        spread = lax.all_to_all(spread, "dp", 0, 0, tiled=True)
        gain_sum = jnp.sum(spread, axis=0)
        gain_sum = (gain_sum + core_swap(gain_sum)).reshape(-1)

        weighted_one = grad_normed_one * gain_one
        grad_input = grad_hidden + scale_one * (
            weighted_one - unit_one * jnp.mean(weighted_one * unit_one, axis=-1, keepdims=True)
        )

        def columns(grads, lo, hi):
            return grads[:, :, lo:hi].reshape(rows, -1)

        return (
            block_out,
            grad_input,
            gain_sum[:width],
            columns(attn_grads, 0, 2 * HD),
            columns(attn_grads, 2 * HD, 3 * HD),
            columns(attn_grads, 3 * HD, 4 * HD),
            columns(attn_grads, 4 * HD, 6 * HD).T,
            gain_sum[2 * width : 2 * width + HD],
            gain_sum[2 * width + HD :],
            gain_sum[width : 2 * width],
            columns(ffn_grads, 0, units),
            columns(ffn_grads, units, 2 * units),
            columns(ffn_grads, 2 * units, 3 * units).T,
        )

    in_specs = (
        P(("dp", "tensor"), None),
        P("dp", None),
        P("dp", None),
        P(),
        P("dp", "tensor"),
        P("dp", "tensor"),
        P("dp", "tensor"),
        P("tensor", "dp"),
        P(),
        P(),
        P(),
        P("dp", "tensor"),
        P("dp", "tensor"),
        P("tensor", "dp"),
        P(("dp", "tensor"), None),
    )
    out_specs = (
        P(("dp", "tensor"), None),
        P(("dp", "tensor"), None),
        P(),
        P("dp", "tensor"),
        P("dp", "tensor"),
        P("dp", "tensor"),
        P("tensor", "dp"),
        P(),
        P(),
        P(),
        P("dp", "tensor"),
        P("dp", "tensor"),
        P("tensor", "dp"),
    )
    return jax.shard_map(body, mesh=mesh, in_specs=in_specs, out_specs=out_specs, check_vma=False)
```

```python
import jax
import jax.numpy as jnp
from jax import lax
from jax.experimental import pallas as pl
from jax.experimental.pallas import tpu as pltpu
from jax.sharding import PartitionSpec as P

HD = 64
PLANE = 4

epsilon = 1e-05
rope_base = 1000000.0
masked_score = -1e30

f32 = jnp.float32
bf16 = jnp.bfloat16

SMALL_COST = pl.CostEstimate(flops=1_000_000, transcendentals=0, bytes_accessed=100_000)


def inverse_rms(values):
    return lax.rsqrt(jnp.mean(values * values, axis=-1, keepdims=True) + epsilon)


def dot_nn(a, b):
    return lax.dot_general(a, b, (((1,), (0,)), ((), ())), preferred_element_type=f32)


def dot_nt(a, b):
    return lax.dot_general(a, b, (((1,), (1,)), ((), ())), preferred_element_type=f32)


def dot_tn(a, b):
    return lax.dot_general(a, b, (((0,), (0,)), ((), ())), preferred_element_type=f32)


def swap_halves(values):
    half = values.shape[-1] // 2
    return jnp.concatenate([values[:, half:], values[:, :half]], axis=-1)


def rope_tables(positions, head_width):
    half_width = head_width // 2
    freq_index = jnp.arange(half_width).astype(f32)
    frequency = rope_base ** (-(2.0 * freq_index) / head_width)
    angles = positions.astype(f32)[..., None] * frequency
    cosine, sine = jnp.cos(angles), jnp.sin(angles)
    return (
        jnp.concatenate([cosine, cosine], axis=-1),
        jnp.concatenate([-sine, sine], axis=-1),
    )


def attention_forward_kernel(
    core_ref,
    own_ref,
    other_ref,
    cos_ref,
    sin_ref,
    seg_col_ref,
    seg_row_ref,
    gain_ref,
    o_own_ref,
    o_other_ref,
    p_ref,
    qkv_ref,
    o_ref,
):
    length = cos_ref.shape[1]
    half = length // 2
    own_rows = pl.ds(pl.multiple_of(core_ref[0] * half, half), half)
    other_rows = pl.ds(pl.multiple_of((1 - core_ref[0]) * half, half), half)
    qkv_ref[own_rows, :] = own_ref[0]
    qkv_ref[other_rows, :] = other_ref[0]
    qkv = qkv_ref[...]
    cosine, sine = cos_ref[0], sin_ref[0]
    row = lax.broadcasted_iota(jnp.int32, (length, length), 0)
    col = lax.broadcasted_iota(jnp.int32, (length, length), 1)
    allowed = (col <= row) & (seg_col_ref[0] == seg_row_ref[0])

    def rotated(lo, gain):
        raw = qkv[:, lo : lo + HD]
        normed = raw * inverse_rms(raw) * gain
        return (normed * cosine + swap_halves(normed) * sine).astype(bf16)

    key = rotated(2 * HD, gain_ref[1:2, :])
    value = qkv[:, 3 * HD : 4 * HD].astype(bf16)
    outs = []
    for head in range(2):
        query = rotated(head * HD, gain_ref[0:1, :])
        scores = jnp.where(allowed, dot_nt(query, key) * HD**-0.5, masked_score)
        row_max = jnp.max(scores, axis=-1, keepdims=True)
        raised = jnp.exp(scores - row_max)
        total = jnp.sum(raised, axis=-1, keepdims=True)
        weights = (raised * (1.0 / total)).astype(bf16)
        p_ref[0, head] = weights
        outs.append(dot_nn(weights, value))
    o_ref[...] = jnp.concatenate(outs, axis=-1)
    o_own_ref[0] = o_ref[own_rows, :].astype(bf16)
    o_other_ref[0] = o_ref[other_rows, :].astype(bf16)


def attention_backward_kernel(
    core_ref,
    own_ref,
    other_ref,
    do_own_ref,
    do_other_ref,
    cos_ref,
    sin_ref,
    gain_ref,
    p_ref,
    d_own_ref,
    d_other_ref,
    dgain_ref,
    qkv_ref,
    do_ref,
):
    length = cos_ref.shape[1]
    half = length // 2
    own_rows = pl.ds(pl.multiple_of(core_ref[0] * half, half), half)
    other_rows = pl.ds(pl.multiple_of((1 - core_ref[0]) * half, half), half)
    qkv_ref[own_rows, :] = own_ref[0]
    qkv_ref[other_rows, :] = other_ref[0]
    do_ref[own_rows, :] = do_own_ref[0].astype(f32)
    do_ref[other_rows, :] = do_other_ref[0].astype(f32)
    qkv = qkv_ref[...]
    cosine, sine = cos_ref[0], sin_ref[0]
    grad_o = do_ref[...].astype(bf16)

    def forward(lo, gain):
        raw = qkv[:, lo : lo + HD]
        scale = inverse_rms(raw)
        unit = raw * scale
        normed = unit * gain
        return unit, scale, (normed * cosine + swap_halves(normed) * sine).astype(bf16)

    def backward(grad_rot, unit, scale, gain):
        grad_normed = grad_rot * cosine - swap_halves(grad_rot) * sine
        gain_part = jnp.sum(unit * grad_normed, axis=0, keepdims=True)
        weighted = grad_normed * gain
        mean = jnp.mean(weighted * unit, axis=-1, keepdims=True)
        return scale * (weighted - unit * mean), gain_part

    query_gain, key_gain = gain_ref[0:1, :], gain_ref[1:2, :]
    key_unit, key_scale, key = forward(2 * HD, key_gain)
    value = qkv[:, 3 * HD : 4 * HD].astype(bf16)
    grad_key = jnp.zeros((length, HD), f32)
    grad_value = jnp.zeros((length, HD), f32)
    query_gain_part = jnp.zeros((1, HD), f32)
    parts = []
    for head in range(2):
        query_unit, query_scale, query = forward(head * HD, query_gain)
        low = p_ref[0, head]
        wide = low.astype(f32)
        grad_head = grad_o[:, head * HD : (head + 1) * HD]
        grad_weights = dot_nt(grad_head, value)
        delta = jnp.sum(wide * grad_weights, axis=-1, keepdims=True)
        grad_scores = (wide * (grad_weights - delta) * HD**-0.5).astype(bf16)
        grad_value += dot_tn(low, grad_head)
        grad_key += dot_tn(grad_scores, query)
        part, gain_part = backward(dot_nn(grad_scores, key), query_unit, query_scale, query_gain)
        query_gain_part += gain_part
        parts.append(part)
    part, key_gain_part = backward(grad_key, key_unit, key_scale, key_gain)
    parts += [part, grad_value]
    qkv_ref[...] = jnp.concatenate(parts, axis=-1)
    d_own_ref[0] = qkv_ref[own_rows, :].astype(bf16)
    d_other_ref[0] = qkv_ref[other_rows, :].astype(bf16)
    dgain_ref[0] = jnp.concatenate([query_gain_part, key_gain_part], axis=-1)


def seq_block(*shape):
    return pl.BlockSpec((1,) + shape, lambda s, c: (s,) + (0,) * len(shape))


def attention_forward(core, own, other, cosine, sine, seg_col, seg_row, gains):
    seqs, half, width = own.shape
    length = 2 * half
    return pl.pallas_call(
        attention_forward_kernel,
        grid_spec=pltpu.PrefetchScalarGridSpec(
            num_scalar_prefetch=1,
            grid=(seqs,),
            in_specs=[
                seq_block(half, width),
                seq_block(half, width),
                seq_block(length, HD),
                seq_block(length, HD),
                seq_block(length, 1),
                seq_block(1, length),
                pl.BlockSpec((2, HD), lambda s, c: (0, 0)),
            ],
            out_specs=[
                seq_block(half, 2 * HD),
                seq_block(half, 2 * HD),
                seq_block(2, length, length),
            ],
            scratch_shapes=[
                pltpu.VMEM((length, width), f32),
                pltpu.VMEM((length, 2 * HD), f32),
            ],
        ),
        out_shape=[
            jax.ShapeDtypeStruct((seqs, half, 2 * HD), bf16),
            jax.ShapeDtypeStruct((seqs, half, 2 * HD), bf16),
            jax.ShapeDtypeStruct((seqs, 2, length, length), bf16),
        ],
        cost_estimate=SMALL_COST,
        name="attention_forward",
    )(core, own, other, cosine, sine, seg_col, seg_row, gains)


def attention_backward(core, own, other, do_own, do_other, cosine, sine, gains, weights):
    seqs, half, width = own.shape
    length = 2 * half
    return pl.pallas_call(
        attention_backward_kernel,
        grid_spec=pltpu.PrefetchScalarGridSpec(
            num_scalar_prefetch=1,
            grid=(seqs,),
            in_specs=[
                seq_block(half, width),
                seq_block(half, width),
                seq_block(half, 2 * HD),
                seq_block(half, 2 * HD),
                seq_block(length, HD),
                seq_block(length, HD),
                pl.BlockSpec((2, HD), lambda s, c: (0, 0)),
                seq_block(2, length, length),
            ],
            out_specs=[
                seq_block(half, width),
                seq_block(half, width),
                seq_block(1, 2 * HD),
            ],
            scratch_shapes=[
                pltpu.VMEM((length, width), f32),
                pltpu.VMEM((length, 2 * HD), f32),
            ],
        ),
        out_shape=[
            jax.ShapeDtypeStruct((seqs, half, width), bf16),
            jax.ShapeDtypeStruct((seqs, half, width), bf16),
            jax.ShapeDtypeStruct((seqs, 1, 2 * HD), f32),
        ],
        cost_estimate=SMALL_COST,
        name="attention_backward",
    )(core, own, other, do_own, do_other, cosine, sine, gains, weights)


def ffn_kernel(n_ref, g_ref, w_ref, dn_ref, y_ref, z_ref, gate_ref, up_ref):
    depth, _, band = w_ref.shape
    units = z_ref.shape[1]

    def over_width(x_ref, lo):
        total = None
        for i in range(depth):
            part = dot_nt(x_ref[:, i * band : (i + 1) * band], w_ref[i, lo : lo + units, :])
            total = part if total is None else total + part
        return total

    gate = over_width(n_ref, 0)
    up = over_width(n_ref, units)
    grad_act = over_width(g_ref, 2 * units)
    sigmoid = 1.0 / (1.0 + jnp.exp(-gate))
    silu = gate * sigmoid
    activated = (silu * up).astype(bf16)
    grad_gate = (grad_act * up * sigmoid * (1.0 + gate * (1.0 - sigmoid))).astype(bf16)
    grad_up = (grad_act * silu).astype(bf16)
    for i in range(depth):
        dn_ref[:, i * band : (i + 1) * band] = (
            dot_nn(grad_gate, w_ref[i, :units, :]) + dot_nn(grad_up, w_ref[i, units : 2 * units, :])
        ).astype(dn_ref.dtype)
    z_ref[...] = activated
    gate_ref[...] = grad_gate
    up_ref[...] = grad_up
    for i in range(depth):
        y_ref[:, i * band : (i + 1) * band] = dot_nn(
            activated, w_ref[i, 2 * units :, :]
        ).astype(y_ref.dtype)


def ffn_half(normed, grads, weights, kind):
    tokens, width = normed.shape
    if weights.shape[2] % 128:
        weights = jnp.moveaxis(weights, 0, 1).reshape(1, weights.shape[1], width)
    units = weights.shape[1] // 3
    tile = tokens // 2

    def rows_of(n):
        return pl.BlockSpec((tile, n), lambda i: (i, 0))

    return pl.pallas_call(
        ffn_kernel,
        grid=(tokens // tile,),
        in_specs=[
            rows_of(width),
            rows_of(width),
            pl.BlockSpec(weights.shape, lambda i: (0, 0, 0)),
        ],
        out_specs=[rows_of(width)] * 2 + [rows_of(units)] * 3,
        out_shape=[jax.ShapeDtypeStruct((tokens, width), kind)] * 2
        + [jax.ShapeDtypeStruct((tokens, units), bf16)] * 3,
        compiler_params=pltpu.CompilerParams(vmem_limit_bytes=48 << 20),
        cost_estimate=SMALL_COST,
        name="ffn_half",
    )(normed, grads, weights)


def ffn_grads_kernel(
    n0_ref, n1_ref, g0_ref, g1_ref, a0_ref, a1_ref, u0_ref, u1_ref, z0_ref, z1_ref, out_ref
):
    units = z0_ref.shape[1]

    def product(x0, x1, y0, y1):
        return (dot_tn(x0[...], y0[...]) + dot_tn(x1[...], y1[...])).astype(bf16)

    out_ref[:, :units] = product(n0_ref, n1_ref, a0_ref, a1_ref)
    out_ref[:, units : 2 * units] = product(n0_ref, n1_ref, u0_ref, u1_ref)
    out_ref[:, 2 * units :] = product(g0_ref, g1_ref, z0_ref, z1_ref)


def ffn_grads_call(normed, grads, gates, ups, activated):
    tokens, width = normed[0].shape
    units = activated[0].shape[1]
    tile = width // 4
    slab = pl.BlockSpec((tokens, tile), lambda i: (0, i))
    whole = pl.BlockSpec((tokens, units), lambda i: (0, 0))
    return pl.pallas_call(
        ffn_grads_kernel,
        grid=(width // tile,),
        in_specs=[slab] * 4 + [whole] * 6,
        out_specs=pl.BlockSpec((tile, 3 * units), lambda i: (i, 0)),
        out_shape=jax.ShapeDtypeStruct((width, 3 * units), bf16),
        compiler_params=pltpu.CompilerParams(vmem_limit_bytes=48 << 20),
        cost_estimate=SMALL_COST,
        name="ffn_grads",
    )(*normed, *grads, *gates, *ups, *activated)


def unxor(blocks, index):
    step = 1
    while step < len(blocks):
        odd = (index & step) != 0
        blocks = [
            jnp.where(odd, blocks[k ^ step], blocks[k]) for k in range(len(blocks))
        ]
        step *= 2
    return blocks


def pick(stacked, index):
    return lax.dynamic_index_in_dim(stacked, index, 0, keepdims=False)


def after(value, *others):
    return lax.optimization_barrier((value,) + others)[0]


def solution(mesh):
    devices = mesh.shape["dp"]
    depth = devices // PLANE
    lines = [[place + PLANE * k for k in range(depth)] for place in range(PLANE)]

    def dp_swap(value, mask):
        return lax.ppermute(value, "dp", [(i, i ^ mask) for i in range(devices)])

    def core_swap(value):
        return lax.ppermute(value, "tensor", [(0, 1), (1, 0)])

    def body(
        block_input,
        segments,
        positions,
        norm1_gain,
        w_query,
        w_key,
        w_value,
        w_out,
        query_gain,
        key_gain,
        norm2_gain,
        w_gate,
        w_up,
        w_down,
        grad_out,
    ):
        me = lax.axis_index("dp")
        core = lax.axis_index("tensor")
        place, level = me % PLANE, me // PLANE
        half, width = block_input.shape
        length = 2 * half
        rows = w_query.shape[0]
        band = PLANE * rows
        units = w_gate.shape[1] // PLANE

        def quarters(*arrays):
            parts = [jnp.moveaxis(a.reshape(rows, PLANE, -1), 1, 0) for a in arrays]
            return jnp.concatenate(parts, axis=-1)

        def plane_exchange(stacked):
            received = [pick(stacked, place)]
            for k in range(1, PLANE):
                received.append(dp_swap(pick(stacked, place ^ k), k))
            return jnp.stack(unxor(received, place))

        def gather_chips(block):
            return jnp.concatenate([block] + [dp_swap(block, k) for k in range(1, PLANE)], axis=0)

        def reduce_chips(mine):
            mine = mine.reshape(PLANE, half, width)
            total = mine[0]
            for k in range(1, PLANE):
                total += dp_swap(mine[k].astype(bf16), k).astype(f32)
            return total

        gain_one = norm1_gain.astype(f32)
        gain_two = norm2_gain.astype(f32)
        head_gains = jnp.stack([query_gain, key_gain]).astype(f32)
        core_index = core.astype(jnp.int32).reshape(1)

        own_x = gather_chips(block_input)
        attn_stack = quarters(w_query, w_key, w_value, w_out.T)
        attn_width = attn_stack.shape[-1]
        layout = jnp.concatenate([segments[0], positions[0] // 256, positions[0] % 256])
        layout_rows = -(-layout.shape[0] // attn_width)
        layout = jnp.pad(layout, (0, layout_rows * attn_width - layout.shape[0]))
        layout = layout.astype(bf16).reshape(layout_rows, attn_width)
        layout_all = jnp.broadcast_to(layout, (PLANE,) + layout.shape)
        attn_stack = jnp.concatenate([attn_stack, layout_all], axis=1)
        received = [pick(attn_stack, place)]
        for k in range(1, PLANE):
            received.append(dp_swap(pick(attn_stack, place ^ k), k))
        layouts = jnp.stack([r[rows:] for r in received]).reshape(PLANE, -1)
        layouts = layouts[:, : 3 * length].astype(f32).reshape(PLANE, 3, length)
        attn_band = jnp.concatenate(unxor([r[:rows] for r in received], place), axis=0)
        attn_band = after(attn_band, own_x)
        ffn_stack = after(quarters(w_gate, w_up, w_down.T), own_x)
        ffn_band = plane_exchange(ffn_stack).reshape(band, 3 * units).T
        bands = [attn_band] + [dp_swap(attn_band, k * PLANE) for k in range(1, depth)]
        attn_weights = jnp.concatenate(unxor(bands, level), axis=0)
        other_x = core_swap(own_x)

        attn_weights = after(attn_weights, ffn_band)
        ffn_weights = lax.all_gather(ffn_band, "dp", axis_index_groups=lines)
        own_go = gather_chips(after(grad_out, ffn_band))

        w_qkv, w_out_t = attn_weights[:, : 4 * HD], attn_weights[:, 4 * HD :]

        def units_of(block):
            wide = block.astype(f32)
            return wide * inverse_rms(wide)

        x_pair = (own_x, other_x)
        n1_pair = [(units_of(x) * gain_one).astype(bf16) for x in x_pair]
        qkv_pair = [dot_nn(n, w_qkv).reshape(PLANE, half, 4 * HD) for n in n1_pair]
        cosine, sine = rope_tables(layouts[:, 1] * 256.0 + layouts[:, 2], HD)
        seg_row, seg_col = layouts[:, 0:1], layouts[:, 0, :, None]
        o_own, o_other, weights = attention_forward(
            core_index, *qkv_pair, cosine, sine, seg_col, seg_row, head_gains
        )
        o_own, o_other = o_own.reshape(-1, 2 * HD), o_other.reshape(-1, 2 * HD)
        o_other = after(o_other, own_go)
        own_go = after(own_go, o_own)
        other_go = core_swap(own_go)

        own_input = block_input.astype(f32)
        scale_one = inverse_rms(own_input)
        unit_one = own_input * scale_one
        sent = core_swap(dot_nt(o_other, w_out_t).astype(bf16))
        hidden = own_input + reduce_chips(dot_nt(o_own, w_out_t) + sent.astype(f32))
        scale_two = inverse_rms(hidden)
        unit_two = hidden * scale_two
        normed_two = (unit_two * gain_two).astype(bf16)
        own_n2 = gather_chips(normed_two)
        other_n2 = core_swap(own_n2)

        dn_other, y_other, z_other, a_other, u_other = ffn_half(
            other_n2, other_go, ffn_weights, bf16
        )
        sent = core_swap(dn_other)
        dn_own, y_own, z_own, a_own, u_own = ffn_half(own_n2, own_go, ffn_weights, f32)
        grad_normed_two = reduce_chips(dn_own + sent.astype(f32))

        ffn_partial = ffn_grads_call(
            (own_n2, other_n2),
            (own_go, other_go),
            (a_own, a_other),
            (u_own, u_other),
            (z_own, z_other),
        )
        ffn_total = lax.psum_scatter(
            ffn_partial.reshape(depth, band, 3 * units), "dp", axis_index_groups=lines
        )

        gain_two_part = jnp.sum(unit_two * grad_normed_two, axis=0)
        weighted_two = grad_normed_two * gain_two
        grad_hidden = grad_out.astype(f32) + scale_two * (
            weighted_two - unit_two * jnp.mean(weighted_two * unit_two, axis=-1, keepdims=True)
        )
        grad_hidden = after(grad_hidden, ffn_partial)
        own_dh = gather_chips(grad_hidden.astype(bf16))
        other_dh = core_swap(own_dh)

        y_sum = after(y_own + core_swap(y_other).astype(f32), own_dh)
        block_out = (hidden + reduce_chips(y_sum)).astype(bf16)

        do_pair = [
            dot_nn(dh, w_out_t).astype(bf16).reshape(PLANE, half, 2 * HD)
            for dh in (own_dh, other_dh)
        ]
        dqkv_own, dqkv_other, head_gain_parts = attention_backward(
            core_index, *qkv_pair, *do_pair, cosine, sine, head_gains, weights
        )
        dqkv_own = after(dqkv_own, block_out).reshape(-1, 4 * HD)
        dqkv_other = dqkv_other.reshape(-1, 4 * HD)

        ffn_total = after(ffn_total, dqkv_own).reshape(PLANE, rows, 3 * units)
        ffn_grads = jnp.moveaxis(plane_exchange(ffn_total), 0, 1).astype(f32)


        sent = core_swap(dot_nt(dqkv_other, w_qkv).astype(bf16))
        dn1_own = dot_nt(dqkv_own, w_qkv)
        dn1_sum = dn1_own + sent.astype(f32)
        grad_normed_one = reduce_chips(dn1_sum)
        attn_partial = jnp.concatenate(
            [
                dot_tn(n1_pair[0], dqkv_own) + dot_tn(n1_pair[1], dqkv_other),
                dot_tn(own_dh, o_own) + dot_tn(other_dh, o_other),
            ],
            axis=-1,
        ).astype(bf16).reshape(depth, band, attn_width)

        gain_one_part = jnp.sum(units_of(own_x) * dn1_sum, axis=0)
        gain_parts = jnp.concatenate(
            [gain_one_part, gain_two_part, jnp.sum(head_gain_parts, axis=(0, 1))]
        )
        gain_count = gain_parts.shape[0]
        gain_rows = -(-gain_count // attn_width)

        def two_parts(sums):
            high = sums.astype(bf16)
            return jnp.concatenate([high, (sums - high.astype(f32)).astype(bf16)], axis=0)

        def joined(extra):
            extra = extra.astype(f32)
            return extra[:gain_rows] + extra[gain_rows:]

        gain_sum = jnp.pad(gain_parts, (0, gain_rows * attn_width - gain_count))
        gain_sum = gain_sum.reshape(gain_rows, attn_width)
        extra = two_parts(gain_sum)
        total = pick(attn_partial, level).astype(f32)
        for k in range(1, depth):
            message = jnp.concatenate([pick(attn_partial, level ^ k), extra], axis=0)
            message = dp_swap(message, k * PLANE)
            total += message[:band].astype(f32)
            gain_sum += joined(message[band:])
        total = total.astype(bf16).reshape(PLANE, rows, attn_width)
        extra = two_parts(gain_sum)
        received = [pick(total, place)]
        for k in range(1, PLANE):
            message = jnp.concatenate([pick(total, place ^ k), extra], axis=0)
            message = dp_swap(message, k)
            received.append(message[:rows])
            gain_sum += joined(message[rows:])
        attn_grads = jnp.stack(unxor(received, place), axis=1).astype(f32)
        gain_sum = (gain_sum + core_swap(gain_sum)).reshape(-1)

        weighted_one = grad_normed_one * gain_one
        grad_input = grad_hidden + scale_one * (
            weighted_one - unit_one * jnp.mean(weighted_one * unit_one, axis=-1, keepdims=True)
        )

        def columns(grads, lo, hi):
            return grads[:, :, lo:hi].reshape(rows, -1)

        return (
            block_out,
            grad_input,
            gain_sum[:width],
            columns(attn_grads, 0, 2 * HD),
            columns(attn_grads, 2 * HD, 3 * HD),
            columns(attn_grads, 3 * HD, 4 * HD),
            columns(attn_grads, 4 * HD, 6 * HD).T,
            gain_sum[2 * width : 2 * width + HD],
            gain_sum[2 * width + HD : 2 * width + 2 * HD],
            gain_sum[width : 2 * width],
            columns(ffn_grads, 0, units),
            columns(ffn_grads, units, 2 * units),
            columns(ffn_grads, 2 * units, 3 * units).T,
        )

    in_specs = (
        P(("dp", "tensor"), None),
        P("dp", None),
        P("dp", None),
        P(),
        P("dp", "tensor"),
        P("dp", "tensor"),
        P("dp", "tensor"),
        P("tensor", "dp"),
        P(),
        P(),
        P(),
        P("dp", "tensor"),
        P("dp", "tensor"),
        P("tensor", "dp"),
        P(("dp", "tensor"), None),
    )
    out_specs = (
        P(("dp", "tensor"), None),
        P(("dp", "tensor"), None),
        P(),
        P("dp", "tensor"),
        P("dp", "tensor"),
        P("dp", "tensor"),
        P("tensor", "dp"),
        P(),
        P(),
        P(),
        P("dp", "tensor"),
        P("dp", "tensor"),
        P("tensor", "dp"),
    )
    return jax.shard_map(body, mesh=mesh, in_specs=in_specs, out_specs=out_specs, check_vma=False)
```

```python
import jax
import jax.numpy as jnp
from jax import lax
from jax.experimental.layout import Layout, with_layout_constraint
from jax.experimental import pallas as pl
from jax.experimental.pallas import tpu as pltpu
from jax.sharding import PartitionSpec as P

HD = 64
PLANE = 4

epsilon = 1e-05
rope_base = 1000000.0
masked_score = -1e30

f32 = jnp.float32
bf16 = jnp.bfloat16

SMALL_COST = pl.CostEstimate(flops=1_000_000, transcendentals=0, bytes_accessed=100_000)


def inverse_rms(values):
    return lax.rsqrt(jnp.mean(values * values, axis=-1, keepdims=True) + epsilon)


def dot_nn(a, b):
    return lax.dot_general(a, b, (((1,), (0,)), ((), ())), preferred_element_type=f32)


def dot_nt(a, b):
    return lax.dot_general(a, b, (((1,), (1,)), ((), ())), preferred_element_type=f32)


def dot_tn(a, b):
    return lax.dot_general(a, b, (((0,), (0,)), ((), ())), preferred_element_type=f32)


def swap_halves(values):
    half = values.shape[-1] // 2
    return jnp.concatenate([values[:, half:], values[:, :half]], axis=-1)


def rope_tables(positions, head_width):
    half_width = head_width // 2
    freq_index = jnp.arange(half_width).astype(f32)
    frequency = rope_base ** (-(2.0 * freq_index) / head_width)
    angles = positions.astype(f32)[..., None] * frequency
    cosine, sine = jnp.cos(angles), jnp.sin(angles)
    return (
        jnp.concatenate([cosine, cosine], axis=-1),
        jnp.concatenate([-sine, sine], axis=-1),
    )


def attention_forward_kernel(
    core_ref,
    own_ref,
    other_ref,
    cos_ref,
    sin_ref,
    seg_col_ref,
    seg_row_ref,
    gain_ref,
    o_own_ref,
    o_other_ref,
    p_ref,
    qkv_ref,
    o_ref,
):
    length = cos_ref.shape[1]
    half = length // 2
    own_rows = pl.ds(pl.multiple_of(core_ref[0] * half, half), half)
    other_rows = pl.ds(pl.multiple_of((1 - core_ref[0]) * half, half), half)
    qkv_ref[own_rows, :] = own_ref[0]
    qkv_ref[other_rows, :] = other_ref[0]
    qkv = qkv_ref[...]
    cosine, sine = cos_ref[0], sin_ref[0]
    row = lax.broadcasted_iota(jnp.int32, (length, length), 0)
    col = lax.broadcasted_iota(jnp.int32, (length, length), 1)
    allowed = (col <= row) & (seg_col_ref[0] == seg_row_ref[0])

    def rotated(lo, gain):
        raw = qkv[:, lo : lo + HD]
        normed = raw * inverse_rms(raw) * gain
        return (normed * cosine + swap_halves(normed) * sine).astype(bf16)

    key = rotated(2 * HD, gain_ref[1:2, :])
    value = qkv[:, 3 * HD : 4 * HD].astype(bf16)
    outs = []
    for head in range(2):
        query = rotated(head * HD, gain_ref[0:1, :])
        scores = jnp.where(allowed, dot_nt(query, key) * HD**-0.5, masked_score)
        row_max = jnp.max(scores, axis=-1, keepdims=True)
        raised = jnp.exp(scores - row_max)
        total = jnp.sum(raised, axis=-1, keepdims=True)
        weights = (raised * (1.0 / total)).astype(bf16)
        p_ref[0, head] = weights
        outs.append(dot_nn(weights, value))
    o_ref[...] = jnp.concatenate(outs, axis=-1)
    o_own_ref[0] = o_ref[own_rows, :].astype(bf16)
    o_other_ref[0] = o_ref[other_rows, :].astype(bf16)


def attention_backward_kernel(
    core_ref,
    own_ref,
    other_ref,
    do_own_ref,
    do_other_ref,
    cos_ref,
    sin_ref,
    gain_ref,
    p_ref,
    d_own_ref,
    d_other_ref,
    dgain_ref,
    qkv_ref,
    do_ref,
):
    length = cos_ref.shape[1]
    half = length // 2
    own_rows = pl.ds(pl.multiple_of(core_ref[0] * half, half), half)
    other_rows = pl.ds(pl.multiple_of((1 - core_ref[0]) * half, half), half)
    qkv_ref[own_rows, :] = own_ref[0]
    qkv_ref[other_rows, :] = other_ref[0]
    do_ref[own_rows, :] = do_own_ref[0].astype(f32)
    do_ref[other_rows, :] = do_other_ref[0].astype(f32)
    qkv = qkv_ref[...]
    cosine, sine = cos_ref[0], sin_ref[0]
    grad_o = do_ref[...].astype(bf16)

    def forward(lo, gain):
        raw = qkv[:, lo : lo + HD]
        scale = inverse_rms(raw)
        unit = raw * scale
        normed = unit * gain
        return unit, scale, (normed * cosine + swap_halves(normed) * sine).astype(bf16)

    def backward(grad_rot, unit, scale, gain):
        grad_normed = grad_rot * cosine - swap_halves(grad_rot) * sine
        gain_part = jnp.sum(unit * grad_normed, axis=0, keepdims=True)
        weighted = grad_normed * gain
        mean = jnp.mean(weighted * unit, axis=-1, keepdims=True)
        return scale * (weighted - unit * mean), gain_part

    query_gain, key_gain = gain_ref[0:1, :], gain_ref[1:2, :]
    key_unit, key_scale, key = forward(2 * HD, key_gain)
    value = qkv[:, 3 * HD : 4 * HD].astype(bf16)
    grad_key = jnp.zeros((length, HD), f32)
    grad_value = jnp.zeros((length, HD), f32)
    query_gain_part = jnp.zeros((1, HD), f32)
    parts = []
    for head in range(2):
        query_unit, query_scale, query = forward(head * HD, query_gain)
        low = p_ref[0, head]
        wide = low.astype(f32)
        grad_head = grad_o[:, head * HD : (head + 1) * HD]
        grad_weights = dot_nt(grad_head, value)
        delta = jnp.sum(wide * grad_weights, axis=-1, keepdims=True)
        grad_scores = (wide * (grad_weights - delta) * HD**-0.5).astype(bf16)
        grad_value += dot_tn(low, grad_head)
        grad_key += dot_tn(grad_scores, query)
        part, gain_part = backward(dot_nn(grad_scores, key), query_unit, query_scale, query_gain)
        query_gain_part += gain_part
        parts.append(part)
    part, key_gain_part = backward(grad_key, key_unit, key_scale, key_gain)
    parts += [part, grad_value]
    qkv_ref[...] = jnp.concatenate(parts, axis=-1)
    d_own_ref[0] = qkv_ref[own_rows, :].astype(bf16)
    d_other_ref[0] = qkv_ref[other_rows, :].astype(bf16)
    dgain_ref[0] = jnp.concatenate([query_gain_part, key_gain_part], axis=-1)


def seq_block(*shape):
    return pl.BlockSpec((1,) + shape, lambda s, c: (s,) + (0,) * len(shape))


def attention_forward(core, own, other, cosine, sine, seg_col, seg_row, gains):
    seqs, half, width = own.shape
    length = 2 * half
    return pl.pallas_call(
        attention_forward_kernel,
        grid_spec=pltpu.PrefetchScalarGridSpec(
            num_scalar_prefetch=1,
            grid=(seqs,),
            in_specs=[
                seq_block(half, width),
                seq_block(half, width),
                seq_block(length, HD),
                seq_block(length, HD),
                seq_block(length, 1),
                seq_block(1, length),
                pl.BlockSpec((2, HD), lambda s, c: (0, 0)),
            ],
            out_specs=[
                seq_block(half, 2 * HD),
                seq_block(half, 2 * HD),
                seq_block(2, length, length),
            ],
            scratch_shapes=[
                pltpu.VMEM((length, width), f32),
                pltpu.VMEM((length, 2 * HD), f32),
            ],
        ),
        out_shape=[
            jax.ShapeDtypeStruct((seqs, half, 2 * HD), bf16),
            jax.ShapeDtypeStruct((seqs, half, 2 * HD), bf16),
            jax.ShapeDtypeStruct((seqs, 2, length, length), bf16),
        ],
        cost_estimate=SMALL_COST,
        name="attention_forward",
    )(core, own, other, cosine, sine, seg_col, seg_row, gains)


def attention_backward(core, own, other, do_own, do_other, cosine, sine, gains, weights):
    seqs, half, width = own.shape
    length = 2 * half
    return pl.pallas_call(
        attention_backward_kernel,
        grid_spec=pltpu.PrefetchScalarGridSpec(
            num_scalar_prefetch=1,
            grid=(seqs,),
            in_specs=[
                seq_block(half, width),
                seq_block(half, width),
                seq_block(half, 2 * HD),
                seq_block(half, 2 * HD),
                seq_block(length, HD),
                seq_block(length, HD),
                pl.BlockSpec((2, HD), lambda s, c: (0, 0)),
                seq_block(2, length, length),
            ],
            out_specs=[
                seq_block(half, width),
                seq_block(half, width),
                seq_block(1, 2 * HD),
            ],
            scratch_shapes=[
                pltpu.VMEM((length, width), f32),
                pltpu.VMEM((length, 2 * HD), f32),
            ],
        ),
        out_shape=[
            jax.ShapeDtypeStruct((seqs, half, width), bf16),
            jax.ShapeDtypeStruct((seqs, half, width), bf16),
            jax.ShapeDtypeStruct((seqs, 1, 2 * HD), f32),
        ],
        cost_estimate=SMALL_COST,
        name="attention_backward",
    )(core, own, other, do_own, do_other, cosine, sine, gains, weights)


def ffn_kernel(n_ref, g_ref, w_ref, dn_ref, y_ref, z_ref, d_ref):
    units = z_ref.shape[1]
    gate_up = dot_nn(n_ref[...], w_ref[:, : 2 * units])
    grad_act = dot_nn(g_ref[...], w_ref[:, 2 * units :])
    gate, up = gate_up[:, :units], gate_up[:, units:]
    sigmoid = 1.0 / (1.0 + jnp.exp(-gate))
    silu = gate * sigmoid
    activated = (silu * up).astype(bf16)
    grad_gate = grad_act * up * sigmoid * (1.0 + gate * (1.0 - sigmoid))
    grad = jnp.concatenate([grad_gate, grad_act * silu], axis=-1).astype(bf16)
    d_ref[...] = grad
    z_ref[...] = activated
    dn_ref[...] = dot_nt(grad, w_ref[:, : 2 * units]).astype(dn_ref.dtype)
    y_ref[...] = dot_nt(activated, w_ref[:, 2 * units :]).astype(y_ref.dtype)


def ffn_half(normed, grads, weights, kind):
    tokens, width = normed.shape
    columns = weights.shape[1]
    units = columns // 3
    tile = tokens // 2

    def rows_of(n):
        return pl.BlockSpec((tile, n), lambda i: (i, 0))

    return pl.pallas_call(
        ffn_kernel,
        grid=(tokens // tile,),
        in_specs=[
            rows_of(width),
            rows_of(width),
            pl.BlockSpec((width, columns), lambda i: (0, 0)),
        ],
        out_specs=[rows_of(width)] * 2 + [rows_of(units), rows_of(2 * units)],
        out_shape=[jax.ShapeDtypeStruct((tokens, width), kind)] * 2
        + [
            jax.ShapeDtypeStruct((tokens, units), bf16),
            jax.ShapeDtypeStruct((tokens, 2 * units), bf16),
        ],
        compiler_params=pltpu.CompilerParams(vmem_limit_bytes=48 << 20),
        cost_estimate=SMALL_COST,
        name="ffn_half",
    )(normed, grads, weights)


def ffn_grads_kernel(n0_ref, n1_ref, g0_ref, g1_ref, d0_ref, d1_ref, z0_ref, z1_ref, out_ref):
    pair = d0_ref.shape[1]

    def product(x0, x1, y0, y1):
        return (dot_tn(x0[...], y0[...]) + dot_tn(x1[...], y1[...])).astype(bf16)

    out_ref[:, :pair] = product(n0_ref, n1_ref, d0_ref, d1_ref)
    out_ref[:, pair:] = product(g0_ref, g1_ref, z0_ref, z1_ref)


def ffn_grads_call(normed, grads, grad_pairs, activated):
    tokens, width = normed[0].shape
    units = activated[0].shape[1]
    tile = width // 4
    slab = pl.BlockSpec((tokens, tile), lambda i: (0, i))

    def whole(n):
        return pl.BlockSpec((tokens, n), lambda i: (0, 0))

    return pl.pallas_call(
        ffn_grads_kernel,
        grid=(width // tile,),
        in_specs=[slab] * 4 + [whole(2 * units)] * 2 + [whole(units)] * 2,
        out_specs=pl.BlockSpec((tile, 3 * units), lambda i: (i, 0)),
        out_shape=jax.ShapeDtypeStruct((width, 3 * units), bf16),
        compiler_params=pltpu.CompilerParams(vmem_limit_bytes=48 << 20),
        cost_estimate=pl.CostEstimate(
            flops=4 * tokens * width * 3 * units,
            transcendentals=0,
            bytes_accessed=4 * tokens * (2 * width + 3 * units) + 6 * width * units,
        ),
        name="ffn_grads",
    )(*normed, *grads, *grad_pairs, *activated)


def unxor(blocks, index):
    step = 1
    while step < len(blocks):
        odd = (index & step) != 0
        blocks = [
            jnp.where(odd, blocks[k ^ step], blocks[k]) for k in range(len(blocks))
        ]
        step *= 2
    return blocks


def pick(stacked, index):
    return lax.dynamic_index_in_dim(stacked, index, 0, keepdims=False)


def after(value, *others):
    return lax.optimization_barrier((value,) + others)[0]


def solution(mesh):
    devices = mesh.shape["dp"]
    depth = devices // PLANE
    lines = [[place + PLANE * k for k in range(depth)] for place in range(PLANE)]

    def dp_swap(value, mask):
        return lax.ppermute(value, "dp", [(i, i ^ mask) for i in range(devices)])

    def core_swap(value):
        return lax.ppermute(value, "tensor", [(0, 1), (1, 0)])

    def body(
        block_input,
        segments,
        positions,
        norm1_gain,
        w_query,
        w_key,
        w_value,
        w_out,
        query_gain,
        key_gain,
        norm2_gain,
        w_gate,
        w_up,
        w_down,
        grad_out,
    ):
        me = lax.axis_index("dp")
        core = lax.axis_index("tensor")
        place, level = me % PLANE, me // PLANE
        half, width = block_input.shape
        length = 2 * half
        rows = w_query.shape[0]
        band = PLANE * rows
        units = w_gate.shape[1] // PLANE

        def quarters(*arrays):
            parts = [jnp.moveaxis(a.reshape(rows, PLANE, -1), 1, 0) for a in arrays]
            return jnp.concatenate(parts, axis=-1)

        def plane_exchange(stacked, *marks):
            received = [pick(stacked, place)]
            for k in range(1, PLANE):
                received.append(after(dp_swap(pick(stacked, place ^ k), k), *marks))
            return jnp.stack(unxor(received, place))

        def gather_chips(block, *marks):
            chips = [block] + [after(dp_swap(block, k), *marks) for k in range(1, PLANE)]
            return jnp.concatenate(chips, axis=0)

        def reduce_chips(mine, *marks):
            mine = mine.reshape(PLANE, half, width)
            total = mine[0]
            for k in range(1, PLANE):
                total += after(dp_swap(mine[k].astype(bf16), k), *marks).astype(f32)
            return total

        gain_one = norm1_gain.astype(f32)
        gain_two = norm2_gain.astype(f32)
        head_gains = jnp.stack([query_gain, key_gain]).astype(f32)
        core_index = core.astype(jnp.int32).reshape(1)

        attn_stack = quarters(w_query, w_key, w_value, w_out.T)
        attn_width = attn_stack.shape[-1]
        layout = jnp.concatenate([segments[0], positions[0] // 256, positions[0] % 256])
        layout_rows = -(-layout.shape[0] // attn_width)
        layout = jnp.pad(layout, (0, layout_rows * attn_width - layout.shape[0]))
        layout = layout.astype(bf16).reshape(layout_rows, attn_width)
        layout_all = jnp.broadcast_to(layout, (PLANE,) + layout.shape)
        attn_stack = jnp.concatenate([attn_stack, layout_all], axis=1)
        received = [pick(attn_stack, place)]
        for k in range(1, PLANE):
            received.append(dp_swap(pick(attn_stack, place ^ k), k))
        layouts = jnp.stack([r[rows:] for r in received]).reshape(PLANE, -1)
        layouts = layouts[:, : 3 * length].astype(f32).reshape(PLANE, 3, length)
        attn_band = jnp.concatenate(unxor([r[:rows] for r in received], place), axis=0)
        ffn_stack = after(quarters(w_gate, w_up, w_down.T), attn_stack)
        ffn_stack = with_layout_constraint(ffn_stack, Layout(major_to_minor=(0, 1, 2)))
        ffn_band = plane_exchange(ffn_stack).reshape(band, 3 * units)
        ffn_weights = lax.all_gather(ffn_band, "dp", axis_index_groups=lines)
        ffn_weights = ffn_weights.reshape(width, 3 * units)

        bands = [attn_band]
        for k in range(1, depth):
            bands.append(dp_swap(attn_band, k * PLANE))
        attn_weights = jnp.concatenate(unxor(bands, level), axis=0)
        own_x = gather_chips(after(block_input, ffn_band))
        other_x = core_swap(own_x)

        w_qkv, w_out_t = attn_weights[:, : 4 * HD], attn_weights[:, 4 * HD :]

        def units_of(block):
            wide = block.astype(f32)
            return wide * inverse_rms(wide)

        x_pair = (own_x, other_x)
        n1_pair = [(units_of(x) * gain_one).astype(bf16) for x in x_pair]
        qkv_pair = [dot_nn(n, w_qkv).reshape(PLANE, half, 4 * HD) for n in n1_pair]
        layouts = after(layouts, ffn_band)
        cosine, sine = rope_tables(layouts[:, 1] * 256.0 + layouts[:, 2], HD)
        seg_row, seg_col = layouts[:, 0:1], layouts[:, 0, :, None]
        o_own, o_other, weights = attention_forward(
            core_index, *qkv_pair, cosine, sine, seg_col, seg_row, head_gains
        )
        o_own, o_other = o_own.reshape(-1, 2 * HD), o_other.reshape(-1, 2 * HD)
        own_go = gather_chips(after(grad_out, attn_weights, own_x), o_own)
        o_other = after(o_other, own_go)
        other_go = core_swap(own_go)

        own_input = block_input.astype(f32)
        scale_one = inverse_rms(own_input)
        unit_one = own_input * scale_one
        sent = core_swap(dot_nt(o_other, w_out_t).astype(bf16))
        hidden = own_input + reduce_chips(dot_nt(o_own, w_out_t) + sent.astype(f32))
        scale_two = inverse_rms(hidden)
        unit_two = hidden * scale_two
        normed_two = (unit_two * gain_two).astype(bf16)
        own_n2 = gather_chips(normed_two)
        other_n2 = core_swap(own_n2)

        dn_other, y_other, z_other, d_other = ffn_half(
            other_n2, other_go, ffn_weights, bf16
        )
        sent = core_swap(dn_other)
        dn_own, y_own, z_own, d_own = ffn_half(after(own_n2, dn_other), own_go, ffn_weights, f32)
        dn_sum = dn_own + sent.astype(f32)
        grad_normed_two = reduce_chips(dn_sum)
        d_own = after(d_own, dn_sum)

        ffn_partial = ffn_grads_call(
            (own_n2, other_n2),
            (own_go, other_go),
            (d_own, d_other),
            (z_own, z_other),
        )
        ffn_total = lax.psum_scatter(
            ffn_partial.reshape(depth, band, 3 * units), "dp", axis_index_groups=lines
        )

        gain_two_part = jnp.sum(unit_two * grad_normed_two, axis=0)
        weighted_two = grad_normed_two * gain_two
        grad_hidden = grad_out.astype(f32) + scale_two * (
            weighted_two - unit_two * jnp.mean(weighted_two * unit_two, axis=-1, keepdims=True)
        )
        grad_hidden = after(grad_hidden, ffn_partial)
        own_dh = gather_chips(grad_hidden.astype(bf16))
        other_dh = core_swap(own_dh)

        y_sum = after(y_own + core_swap(y_other).astype(f32), own_dh)
        block_out = (hidden + reduce_chips(y_sum)).astype(bf16)

        do_pair = [
            dot_nn(dh, w_out_t).astype(bf16).reshape(PLANE, half, 2 * HD)
            for dh in (own_dh, other_dh)
        ]
        dqkv_own, dqkv_other, head_gain_parts = attention_backward(
            core_index, *qkv_pair, *do_pair, cosine, sine, head_gains, weights
        )
        dqkv_own = after(dqkv_own, block_out).reshape(-1, 4 * HD)
        dqkv_other = dqkv_other.reshape(-1, 4 * HD)

        ffn_total = after(ffn_total, dqkv_own)
        sent = core_swap(dot_nt(dqkv_other, w_qkv).astype(bf16))
        dn1_own = dot_nt(dqkv_own, w_qkv)
        dn1_sum = dn1_own + sent.astype(f32)
        attn_partial = jnp.concatenate(
            [
                dot_tn(n1_pair[0], dqkv_own) + dot_tn(n1_pair[1], dqkv_other),
                dot_tn(own_dh, o_own) + dot_tn(other_dh, o_other),
            ],
            axis=-1,
        ).astype(bf16).reshape(depth, band, attn_width)

        gain_one_part = jnp.sum(units_of(own_x) * dn1_sum, axis=0)
        gain_parts = jnp.concatenate(
            [gain_one_part, gain_two_part, jnp.sum(head_gain_parts, axis=(0, 1))]
        )
        gain_count = gain_parts.shape[0]
        gain_rows = -(-gain_count // attn_width)

        def two_parts(sums):
            high = sums.astype(bf16)
            return jnp.concatenate([high, (sums - high.astype(f32)).astype(bf16)], axis=0)

        def joined(extra):
            extra = extra.astype(f32)
            return extra[:gain_rows] + extra[gain_rows:]

        gain_sum = jnp.pad(gain_parts, (0, gain_rows * attn_width - gain_count))
        gain_sum = gain_sum.reshape(gain_rows, attn_width)
        extra = two_parts(gain_sum)
        total = pick(attn_partial, level).astype(f32)
        messages = []
        for k in range(1, depth):
            message = jnp.concatenate([pick(attn_partial, level ^ k), extra], axis=0)
            message = dp_swap(after(message, ffn_total), k * PLANE)
            messages.append(message)
            total += message[:band].astype(f32)
            gain_sum += joined(message[band:])
        ffn_grads = plane_exchange(ffn_total.reshape(PLANE, rows, 3 * units), *messages)
        ffn_grads = jnp.moveaxis(ffn_grads, 0, 1).astype(f32)


        grad_normed_one = reduce_chips(dn1_sum, ffn_grads)
        total = total.astype(bf16).reshape(PLANE, rows, attn_width)
        extra = two_parts(gain_sum)
        received = [pick(total, place)]
        for k in range(1, PLANE):
            message = jnp.concatenate([pick(total, place ^ k), extra], axis=0)
            message = dp_swap(message, k)
            received.append(message[:rows])
            gain_sum += joined(message[rows:])
        attn_grads = jnp.stack(unxor(received, place), axis=1).astype(f32)
        gain_sum = (gain_sum + core_swap(gain_sum)).reshape(-1)

        weighted_one = grad_normed_one * gain_one
        grad_input = grad_hidden + scale_one * (
            weighted_one - unit_one * jnp.mean(weighted_one * unit_one, axis=-1, keepdims=True)
        )

        def columns(grads, lo, hi):
            return grads[:, :, lo:hi].reshape(rows, -1)

        return (
            block_out,
            grad_input,
            gain_sum[:width],
            columns(attn_grads, 0, 2 * HD),
            columns(attn_grads, 2 * HD, 3 * HD),
            columns(attn_grads, 3 * HD, 4 * HD),
            columns(attn_grads, 4 * HD, 6 * HD).T,
            gain_sum[2 * width : 2 * width + HD],
            gain_sum[2 * width + HD : 2 * width + 2 * HD],
            gain_sum[width : 2 * width],
            columns(ffn_grads, 0, units),
            columns(ffn_grads, units, 2 * units),
            columns(ffn_grads, 2 * units, 3 * units).T,
        )

    in_specs = (
        P(("dp", "tensor"), None),
        P("dp", None),
        P("dp", None),
        P(),
        P("dp", "tensor"),
        P("dp", "tensor"),
        P("dp", "tensor"),
        P("tensor", "dp"),
        P(),
        P(),
        P(),
        P("dp", "tensor"),
        P("dp", "tensor"),
        P("tensor", "dp"),
        P(("dp", "tensor"), None),
    )
    out_specs = (
        P(("dp", "tensor"), None),
        P(("dp", "tensor"), None),
        P(),
        P("dp", "tensor"),
        P("dp", "tensor"),
        P("dp", "tensor"),
        P("tensor", "dp"),
        P(),
        P(),
        P(),
        P("dp", "tensor"),
        P("dp", "tensor"),
        P("tensor", "dp"),
    )
    return jax.shard_map(body, mesh=mesh, in_specs=in_specs, out_specs=out_specs, check_vma=False)
```

```python
import jax
import jax.numpy as jnp
from jax import lax
from jax.experimental.layout import Layout, with_layout_constraint
from jax.experimental import pallas as pl
from jax.experimental.pallas import tpu as pltpu
from jax.sharding import PartitionSpec as P

HD = 64
PLANE = 4
STEP = 2

epsilon = 1e-05
rope_base = 1000000.0
masked_score = -1e30

f32 = jnp.float32
bf16 = jnp.bfloat16

SMALL_COST = pl.CostEstimate(flops=1_000_000, transcendentals=0, bytes_accessed=100_000)


def inverse_rms(values):
    return lax.rsqrt(jnp.mean(values * values, axis=-1, keepdims=True) + epsilon)


def dot_nn(a, b):
    return lax.dot_general(a, b, (((1,), (0,)), ((), ())), preferred_element_type=f32)


def dot_nt(a, b):
    return lax.dot_general(a, b, (((1,), (1,)), ((), ())), preferred_element_type=f32)


def dot_tn(a, b):
    return lax.dot_general(a, b, (((0,), (0,)), ((), ())), preferred_element_type=f32)


def swap_halves(values):
    half = values.shape[-1] // 2
    return jnp.concatenate([values[:, half:], values[:, :half]], axis=-1)


def rope_tables(positions, head_width):
    half_width = head_width // 2
    freq_index = jnp.arange(half_width).astype(f32)
    frequency = rope_base ** (-(2.0 * freq_index) / head_width)
    angles = positions.astype(f32)[..., None] * frequency
    cosine, sine = jnp.cos(angles), jnp.sin(angles)
    return (
        jnp.concatenate([cosine, cosine], axis=-1),
        jnp.concatenate([-sine, sine], axis=-1),
    )


def attention_forward_kernel(
    core_ref,
    own_ref,
    other_ref,
    cos_ref,
    sin_ref,
    seg_col_ref,
    seg_row_ref,
    gain_ref,
    o_own_ref,
    o_other_ref,
    p_ref,
    qkv_ref,
    o_ref,
):
    length = cos_ref.shape[1]
    half = length // 2
    own_rows = pl.ds(pl.multiple_of(core_ref[0] * half, half), half)
    other_rows = pl.ds(pl.multiple_of((1 - core_ref[0]) * half, half), half)

    def forward_one(seq):
        qkv_ref[seq, own_rows, :] = own_ref[seq]
        qkv_ref[seq, other_rows, :] = other_ref[seq]
        qkv = qkv_ref[seq]
        cosine, sine = cos_ref[seq], sin_ref[seq]
        row = lax.broadcasted_iota(jnp.int32, (length, length), 0)
        col = lax.broadcasted_iota(jnp.int32, (length, length), 1)
        allowed = (col <= row) & (seg_col_ref[seq] == seg_row_ref[seq])

        def rotated(lo, gain):
            raw = qkv[:, lo : lo + HD]
            normed = raw * inverse_rms(raw) * gain
            return (normed * cosine + swap_halves(normed) * sine).astype(bf16)

        key = rotated(2 * HD, gain_ref[1:2, :])
        value = qkv[:, 3 * HD : 4 * HD].astype(bf16)
        outs = []
        for head in range(2):
            query = rotated(head * HD, gain_ref[0:1, :])
            scores = jnp.where(allowed, dot_nt(query, key) * HD**-0.5, masked_score)
            row_max = jnp.max(scores, axis=-1, keepdims=True)
            raised = jnp.exp(scores - row_max)
            total = jnp.sum(raised, axis=-1, keepdims=True)
            weights = (raised * (1.0 / total)).astype(bf16)
            p_ref[seq, head] = weights
            outs.append(dot_nn(weights, value))
        o_ref[seq] = jnp.concatenate(outs, axis=-1)
        o_own_ref[seq] = o_ref[seq, own_rows, :].astype(bf16)
        o_other_ref[seq] = o_ref[seq, other_rows, :].astype(bf16)

    for seq in range(cos_ref.shape[0]):
        forward_one(seq)


def attention_backward_kernel(
    core_ref,
    own_ref,
    other_ref,
    do_own_ref,
    do_other_ref,
    cos_ref,
    sin_ref,
    gain_ref,
    p_ref,
    d_own_ref,
    d_other_ref,
    dgain_ref,
    qkv_ref,
    do_ref,
):
    length = cos_ref.shape[1]
    half = length // 2
    own_rows = pl.ds(pl.multiple_of(core_ref[0] * half, half), half)
    other_rows = pl.ds(pl.multiple_of((1 - core_ref[0]) * half, half), half)

    def backward_one(seq):
        qkv_ref[seq, own_rows, :] = own_ref[seq]
        qkv_ref[seq, other_rows, :] = other_ref[seq]
        do_ref[seq, own_rows, :] = do_own_ref[seq].astype(f32)
        do_ref[seq, other_rows, :] = do_other_ref[seq].astype(f32)
        qkv = qkv_ref[seq]
        cosine, sine = cos_ref[seq], sin_ref[seq]
        grad_o = do_ref[seq].astype(bf16)

        def forward(lo, gain):
            raw = qkv[:, lo : lo + HD]
            scale = inverse_rms(raw)
            unit = raw * scale
            normed = unit * gain
            return unit, scale, (normed * cosine + swap_halves(normed) * sine).astype(bf16)

        def backward(grad_rot, unit, scale, gain):
            grad_normed = grad_rot * cosine - swap_halves(grad_rot) * sine
            gain_part = jnp.sum(unit * grad_normed, axis=0, keepdims=True)
            weighted = grad_normed * gain
            mean = jnp.mean(weighted * unit, axis=-1, keepdims=True)
            return scale * (weighted - unit * mean), gain_part

        query_gain, key_gain = gain_ref[0:1, :], gain_ref[1:2, :]
        key_unit, key_scale, key = forward(2 * HD, key_gain)
        value = qkv[:, 3 * HD : 4 * HD].astype(bf16)
        grad_key = jnp.zeros((length, HD), f32)
        grad_value = jnp.zeros((length, HD), f32)
        query_gain_part = jnp.zeros((1, HD), f32)
        parts = []
        for head in range(2):
            query_unit, query_scale, query = forward(head * HD, query_gain)
            low = p_ref[seq, head]
            wide = low.astype(f32)
            grad_head = grad_o[:, head * HD : (head + 1) * HD]
            grad_weights = dot_nt(grad_head, value)
            delta = jnp.sum(wide * grad_weights, axis=-1, keepdims=True)
            grad_scores = (wide * (grad_weights - delta) * HD**-0.5).astype(bf16)
            grad_value += dot_tn(low, grad_head)
            grad_key += dot_tn(grad_scores, query)
            part, gain_part = backward(dot_nn(grad_scores, key), query_unit, query_scale, query_gain)
            query_gain_part += gain_part
            parts.append(part)
        part, key_gain_part = backward(grad_key, key_unit, key_scale, key_gain)
        parts += [part, grad_value]
        qkv_ref[seq] = jnp.concatenate(parts, axis=-1)
        d_own_ref[seq] = qkv_ref[seq, own_rows, :].astype(bf16)
        d_other_ref[seq] = qkv_ref[seq, other_rows, :].astype(bf16)
        dgain_ref[seq] = jnp.concatenate([query_gain_part, key_gain_part], axis=-1)

    for seq in range(cos_ref.shape[0]):
        backward_one(seq)


def seq_block(*shape):
    return pl.BlockSpec((STEP,) + shape, lambda s, c: (s,) + (0,) * len(shape))


def attention_forward(core, own, other, cosine, sine, seg_col, seg_row, gains):
    seqs, half, width = own.shape
    length = 2 * half
    return pl.pallas_call(
        attention_forward_kernel,
        grid_spec=pltpu.PrefetchScalarGridSpec(
            num_scalar_prefetch=1,
            grid=(seqs // STEP,),
            in_specs=[
                seq_block(half, width),
                seq_block(half, width),
                seq_block(length, HD),
                seq_block(length, HD),
                seq_block(length, 1),
                seq_block(1, length),
                pl.BlockSpec((2, HD), lambda s, c: (0, 0)),
            ],
            out_specs=[
                seq_block(half, 2 * HD),
                seq_block(half, 2 * HD),
                seq_block(2, length, length),
            ],
            scratch_shapes=[
                pltpu.VMEM((STEP, length, width), f32),
                pltpu.VMEM((STEP, length, 2 * HD), f32),
            ],
        ),
        out_shape=[
            jax.ShapeDtypeStruct((seqs, half, 2 * HD), bf16),
            jax.ShapeDtypeStruct((seqs, half, 2 * HD), bf16),
            jax.ShapeDtypeStruct((seqs, 2, length, length), bf16),
        ],
        compiler_params=pltpu.CompilerParams(vmem_limit_bytes=48 << 20),
        cost_estimate=SMALL_COST,
        name="attention_forward",
    )(core, own, other, cosine, sine, seg_col, seg_row, gains)


def attention_backward(core, own, other, do_own, do_other, cosine, sine, gains, weights):
    seqs, half, width = own.shape
    length = 2 * half
    return pl.pallas_call(
        attention_backward_kernel,
        grid_spec=pltpu.PrefetchScalarGridSpec(
            num_scalar_prefetch=1,
            grid=(seqs // STEP,),
            in_specs=[
                seq_block(half, width),
                seq_block(half, width),
                seq_block(half, 2 * HD),
                seq_block(half, 2 * HD),
                seq_block(length, HD),
                seq_block(length, HD),
                pl.BlockSpec((2, HD), lambda s, c: (0, 0)),
                seq_block(2, length, length),
            ],
            out_specs=[
                seq_block(half, width),
                seq_block(half, width),
                seq_block(1, 2 * HD),
            ],
            scratch_shapes=[
                pltpu.VMEM((STEP, length, width), f32),
                pltpu.VMEM((STEP, length, 2 * HD), f32),
            ],
        ),
        out_shape=[
            jax.ShapeDtypeStruct((seqs, half, width), bf16),
            jax.ShapeDtypeStruct((seqs, half, width), bf16),
            jax.ShapeDtypeStruct((seqs, 1, 2 * HD), f32),
        ],
        compiler_params=pltpu.CompilerParams(vmem_limit_bytes=48 << 20),
        cost_estimate=SMALL_COST,
        name="attention_backward",
    )(core, own, other, do_own, do_other, cosine, sine, gains, weights)


def ffn_kernel(n_ref, g_ref, w_ref, dn_ref, y_ref, z_ref, d_ref):
    units = z_ref.shape[1]
    gate_up = dot_nn(n_ref[...], w_ref[:, : 2 * units])
    grad_act = dot_nn(g_ref[...], w_ref[:, 2 * units :])
    gate, up = gate_up[:, :units], gate_up[:, units:]
    sigmoid = 1.0 / (1.0 + jnp.exp(-gate))
    silu = gate * sigmoid
    activated = (silu * up).astype(bf16)
    grad_gate = grad_act * up * sigmoid * (1.0 + gate * (1.0 - sigmoid))
    grad = jnp.concatenate([grad_gate, grad_act * silu], axis=-1).astype(bf16)
    d_ref[...] = grad
    z_ref[...] = activated
    dn_ref[...] = dot_nt(grad, w_ref[:, : 2 * units]).astype(dn_ref.dtype)
    y_ref[...] = dot_nt(activated, w_ref[:, 2 * units :]).astype(y_ref.dtype)


def ffn_half(normed, grads, weights, kind):
    tokens, width = normed.shape
    columns = weights.shape[1]
    units = columns // 3
    tile = tokens // 2

    def rows_of(n):
        return pl.BlockSpec((tile, n), lambda i: (i, 0))

    return pl.pallas_call(
        ffn_kernel,
        grid=(tokens // tile,),
        in_specs=[
            rows_of(width),
            rows_of(width),
            pl.BlockSpec((width, columns), lambda i: (0, 0)),
        ],
        out_specs=[rows_of(width)] * 2 + [rows_of(units), rows_of(2 * units)],
        out_shape=[jax.ShapeDtypeStruct((tokens, width), kind)] * 2
        + [
            jax.ShapeDtypeStruct((tokens, units), bf16),
            jax.ShapeDtypeStruct((tokens, 2 * units), bf16),
        ],
        compiler_params=pltpu.CompilerParams(vmem_limit_bytes=48 << 20),
        cost_estimate=SMALL_COST,
        name="ffn_half",
    )(normed, grads, weights)


def ffn_grads_kernel(n0_ref, n1_ref, g0_ref, g1_ref, d0_ref, d1_ref, z0_ref, z1_ref, out_ref):
    pair = d0_ref.shape[1]

    def product(x0, x1, y0, y1):
        return (dot_tn(x0[...], y0[...]) + dot_tn(x1[...], y1[...])).astype(bf16)

    out_ref[:, :pair] = product(n0_ref, n1_ref, d0_ref, d1_ref)
    out_ref[:, pair:] = product(g0_ref, g1_ref, z0_ref, z1_ref)


def ffn_grads_call(normed, grads, grad_pairs, activated):
    tokens, width = normed[0].shape
    units = activated[0].shape[1]
    tile = width // 4
    slab = pl.BlockSpec((tokens, tile), lambda i: (0, i))

    def whole(n):
        return pl.BlockSpec((tokens, n), lambda i: (0, 0))

    return pl.pallas_call(
        ffn_grads_kernel,
        grid=(width // tile,),
        in_specs=[slab] * 4 + [whole(2 * units)] * 2 + [whole(units)] * 2,
        out_specs=pl.BlockSpec((tile, 3 * units), lambda i: (i, 0)),
        out_shape=jax.ShapeDtypeStruct((width, 3 * units), bf16),
        compiler_params=pltpu.CompilerParams(vmem_limit_bytes=48 << 20),
        cost_estimate=pl.CostEstimate(
            flops=4 * tokens * width * 3 * units,
            transcendentals=0,
            bytes_accessed=4 * tokens * (2 * width + 3 * units) + 6 * width * units,
        ),
        name="ffn_grads",
    )(*normed, *grads, *grad_pairs, *activated)


def unxor(blocks, index):
    step = 1
    while step < len(blocks):
        odd = (index & step) != 0
        blocks = [
            jnp.where(odd, blocks[k ^ step], blocks[k]) for k in range(len(blocks))
        ]
        step *= 2
    return blocks


def pick(stacked, index):
    return lax.dynamic_index_in_dim(stacked, index, 0, keepdims=False)


def after(value, *others):
    return lax.optimization_barrier((value,) + others)[0]


def solution(mesh):
    devices = mesh.shape["dp"]
    depth = devices // PLANE
    lines = [[place + PLANE * k for k in range(depth)] for place in range(PLANE)]

    def dp_swap(value, mask):
        return lax.ppermute(value, "dp", [(i, i ^ mask) for i in range(devices)])

    def core_swap(value):
        return lax.ppermute(value, "tensor", [(0, 1), (1, 0)])

    def body(
        block_input,
        segments,
        positions,
        norm1_gain,
        w_query,
        w_key,
        w_value,
        w_out,
        query_gain,
        key_gain,
        norm2_gain,
        w_gate,
        w_up,
        w_down,
        grad_out,
    ):
        me = lax.axis_index("dp")
        core = lax.axis_index("tensor")
        place, level = me % PLANE, me // PLANE
        half, width = block_input.shape
        length = 2 * half
        rows = w_query.shape[0]
        band = PLANE * rows
        units = w_gate.shape[1] // PLANE

        def quarters(*arrays):
            parts = [jnp.moveaxis(a.reshape(rows, PLANE, -1), 1, 0) for a in arrays]
            return jnp.concatenate(parts, axis=-1)

        def plane_exchange(stacked, *marks):
            received = [pick(stacked, place)]
            for k in range(1, PLANE):
                received.append(after(dp_swap(pick(stacked, place ^ k), k), *marks))
            return jnp.stack(unxor(received, place))

        def gather_chips(block, *marks):
            chips = [block] + [after(dp_swap(block, k), *marks) for k in range(1, PLANE)]
            return jnp.concatenate(chips, axis=0)

        def reduce_chips(mine, *marks):
            mine = mine.reshape(PLANE, half, width)
            total = mine[0]
            for k in range(1, PLANE):
                total += after(dp_swap(mine[k].astype(bf16), k), *marks).astype(f32)
            return total

        gain_one = norm1_gain.astype(f32)
        gain_two = norm2_gain.astype(f32)
        head_gains = jnp.stack([query_gain, key_gain]).astype(f32)
        core_index = core.astype(jnp.int32).reshape(1)

        attn_stack = quarters(w_query, w_key, w_value, w_out.T)
        attn_width = attn_stack.shape[-1]
        layout = jnp.concatenate([segments[0], positions[0] // 256, positions[0] % 256])
        layout_rows = -(-layout.shape[0] // attn_width)
        layout = jnp.pad(layout, (0, layout_rows * attn_width - layout.shape[0]))
        layout = layout.astype(bf16).reshape(layout_rows, attn_width)
        layout_all = jnp.broadcast_to(layout, (PLANE,) + layout.shape)
        attn_stack = jnp.concatenate([attn_stack, layout_all], axis=1)
        received = [pick(attn_stack, place)]
        for k in range(1, PLANE):
            received.append(dp_swap(pick(attn_stack, place ^ k), k))
        layouts = jnp.stack([r[rows:] for r in received]).reshape(PLANE, -1)
        layouts = layouts[:, : 3 * length].astype(f32).reshape(PLANE, 3, length)
        attn_band = jnp.concatenate(unxor([r[:rows] for r in received], place), axis=0)
        ffn_stack = after(quarters(w_gate, w_up, w_down.T), attn_stack)
        ffn_stack = with_layout_constraint(ffn_stack, Layout(major_to_minor=(0, 1, 2)))
        ffn_band = plane_exchange(ffn_stack).reshape(band, 3 * units)
        ffn_band = with_layout_constraint(ffn_band, Layout(major_to_minor=(0, 1)))
        ffn_weights = lax.all_gather(ffn_band, "dp", axis_index_groups=lines)
        ffn_weights = with_layout_constraint(ffn_weights, Layout(major_to_minor=(0, 1, 2)))
        ffn_weights = ffn_weights.reshape(width, 3 * units)

        bands = [attn_band]
        for k in range(1, depth):
            bands.append(dp_swap(attn_band, k * PLANE))
        attn_weights = jnp.concatenate(unxor(bands, level), axis=0)
        own_x = gather_chips(after(block_input, ffn_band, bands[1]))
        other_x = core_swap(own_x)

        w_qkv, w_out_t = attn_weights[:, : 4 * HD], attn_weights[:, 4 * HD :]

        def units_of(block):
            wide = block.astype(f32)
            return wide * inverse_rms(wide)

        x_pair = (own_x, other_x)
        n1_pair = [(units_of(x) * gain_one).astype(bf16) for x in x_pair]
        qkv_pair = [dot_nn(n, w_qkv).reshape(PLANE, half, 4 * HD) for n in n1_pair]
        layouts = after(layouts, ffn_band)
        cosine, sine = rope_tables(layouts[:, 1] * 256.0 + layouts[:, 2], HD)
        seg_row, seg_col = layouts[:, 0:1], layouts[:, 0, :, None]
        o_own, o_other, weights = attention_forward(
            core_index, *qkv_pair, cosine, sine, seg_col, seg_row, head_gains
        )
        o_own, o_other = o_own.reshape(-1, 2 * HD), o_other.reshape(-1, 2 * HD)
        own_go = gather_chips(after(grad_out, attn_weights, own_x), o_own)
        o_other = after(o_other, own_go)
        other_go = core_swap(own_go)

        own_input = block_input.astype(f32)
        scale_one = inverse_rms(own_input)
        unit_one = own_input * scale_one
        sent = core_swap(dot_nt(o_other, w_out_t).astype(bf16))
        hidden = own_input + reduce_chips(dot_nt(o_own, w_out_t) + sent.astype(f32))
        scale_two = inverse_rms(hidden)
        unit_two = hidden * scale_two
        normed_two = (unit_two * gain_two).astype(bf16)
        own_n2 = gather_chips(normed_two)
        other_n2 = core_swap(own_n2)

        dn_other, y_other, z_other, d_other = ffn_half(
            other_n2, other_go, ffn_weights, bf16
        )
        sent = core_swap(dn_other)
        dn_own, y_own, z_own, d_own = ffn_half(after(own_n2, dn_other), own_go, ffn_weights, f32)
        dn_sum = dn_own + sent.astype(f32)
        grad_normed_two = reduce_chips(dn_sum)
        d_own = after(d_own, dn_sum)

        ffn_partial = ffn_grads_call(
            (own_n2, other_n2),
            (own_go, other_go),
            (d_own, d_other),
            (z_own, z_other),
        )
        ffn_total = lax.psum_scatter(
            ffn_partial.reshape(depth, band, 3 * units), "dp", axis_index_groups=lines
        )

        gain_two_part = jnp.sum(unit_two * grad_normed_two, axis=0)
        weighted_two = grad_normed_two * gain_two
        grad_hidden = grad_out.astype(f32) + scale_two * (
            weighted_two - unit_two * jnp.mean(weighted_two * unit_two, axis=-1, keepdims=True)
        )
        grad_hidden = after(grad_hidden, ffn_partial)
        own_dh = gather_chips(grad_hidden.astype(bf16))
        other_dh = core_swap(own_dh)

        y_sum = after(y_own + core_swap(y_other).astype(f32), own_dh)
        do_pair = [
            dot_nn(dh, w_out_t).astype(bf16).reshape(PLANE, half, 2 * HD)
            for dh in (own_dh, other_dh)
        ]
        dqkv_own, dqkv_other, head_gain_parts = attention_backward(
            core_index, *qkv_pair, *do_pair, cosine, sine, head_gains, weights
        )
        block_out = (hidden + reduce_chips(y_sum, dqkv_own)).astype(bf16)
        dqkv_own = after(dqkv_own, block_out).reshape(-1, 4 * HD)
        dqkv_other = dqkv_other.reshape(-1, 4 * HD)

        ffn_total = after(ffn_total, dqkv_own)
        sent = core_swap(dot_nt(dqkv_other, w_qkv).astype(bf16))
        dn1_own = dot_nt(dqkv_own, w_qkv)
        dn1_sum = dn1_own + sent.astype(f32)
        attn_partial = jnp.concatenate(
            [
                dot_tn(n1_pair[0], dqkv_own) + dot_tn(n1_pair[1], dqkv_other),
                dot_tn(own_dh, o_own) + dot_tn(other_dh, o_other),
            ],
            axis=-1,
        ).astype(bf16).reshape(depth, band, attn_width)

        gain_one_part = jnp.sum(units_of(own_x) * dn1_sum, axis=0)
        gain_parts = jnp.concatenate(
            [gain_one_part, gain_two_part, jnp.sum(head_gain_parts, axis=(0, 1))]
        )
        gain_count = gain_parts.shape[0]
        gain_rows = -(-gain_count // attn_width)

        def two_parts(sums):
            high = sums.astype(bf16)
            return jnp.concatenate([high, (sums - high.astype(f32)).astype(bf16)], axis=0)

        def joined(extra):
            extra = extra.astype(f32)
            return extra[:gain_rows] + extra[gain_rows:]

        gain_sum = jnp.pad(gain_parts, (0, gain_rows * attn_width - gain_count))
        gain_sum = gain_sum.reshape(gain_rows, attn_width)
        extra = two_parts(gain_sum)
        total = pick(attn_partial, level).astype(f32)
        messages = []
        for k in range(1, depth):
            message = jnp.concatenate([pick(attn_partial, level ^ k), extra], axis=0)
            message = dp_swap(after(message, ffn_total), k * PLANE)
            messages.append(message)
            total += message[:band].astype(f32)
            gain_sum += joined(message[band:])
        ffn_grads = plane_exchange(ffn_total.reshape(PLANE, rows, 3 * units), *messages)
        ffn_grads = jnp.moveaxis(ffn_grads, 0, 1).astype(f32)


        grad_normed_one = reduce_chips(dn1_sum, messages[-1])
        total = total.astype(bf16).reshape(PLANE, rows, attn_width)
        extra = two_parts(gain_sum)
        received = [pick(total, place)]
        for k in range(1, PLANE):
            message = jnp.concatenate([pick(total, place ^ k), extra], axis=0)
            message = dp_swap(message, k)
            received.append(message[:rows])
            gain_sum += joined(message[rows:])
        attn_grads = jnp.stack(unxor(received, place), axis=1).astype(f32)
        gain_sum = (gain_sum + core_swap(gain_sum)).reshape(-1)

        weighted_one = grad_normed_one * gain_one
        grad_input = grad_hidden + scale_one * (
            weighted_one - unit_one * jnp.mean(weighted_one * unit_one, axis=-1, keepdims=True)
        )

        def columns(grads, lo, hi):
            return grads[:, :, lo:hi].reshape(rows, -1)

        return (
            block_out,
            grad_input,
            gain_sum[:width],
            columns(attn_grads, 0, 2 * HD),
            columns(attn_grads, 2 * HD, 3 * HD),
            columns(attn_grads, 3 * HD, 4 * HD),
            columns(attn_grads, 4 * HD, 6 * HD).T,
            gain_sum[2 * width : 2 * width + HD],
            gain_sum[2 * width + HD : 2 * width + 2 * HD],
            gain_sum[width : 2 * width],
            columns(ffn_grads, 0, units),
            columns(ffn_grads, units, 2 * units),
            columns(ffn_grads, 2 * units, 3 * units).T,
        )

    in_specs = (
        P(("dp", "tensor"), None),
        P("dp", None),
        P("dp", None),
        P(),
        P("dp", "tensor"),
        P("dp", "tensor"),
        P("dp", "tensor"),
        P("tensor", "dp"),
        P(),
        P(),
        P(),
        P("dp", "tensor"),
        P("dp", "tensor"),
        P("tensor", "dp"),
        P(("dp", "tensor"), None),
    )
    out_specs = (
        P(("dp", "tensor"), None),
        P(("dp", "tensor"), None),
        P(),
        P("dp", "tensor"),
        P("dp", "tensor"),
        P("dp", "tensor"),
        P("tensor", "dp"),
        P(),
        P(),
        P(),
        P("dp", "tensor"),
        P("dp", "tensor"),
        P("tensor", "dp"),
    )
    return jax.shard_map(body, mesh=mesh, in_specs=in_specs, out_specs=out_specs, check_vma=False)
```

```python
import jax
import jax.numpy as jnp
from jax import lax
from jax.experimental.layout import Layout, with_layout_constraint
from jax.experimental import pallas as pl
from jax.experimental.pallas import tpu as pltpu
from jax.sharding import PartitionSpec as P

HD = 64
PLANE = 4
STEP = 2

epsilon = 1e-05
rope_base = 1000000.0
masked_score = -1e30

f32 = jnp.float32
bf16 = jnp.bfloat16

SMALL_COST = pl.CostEstimate(flops=1_000_000, transcendentals=0, bytes_accessed=100_000)


def inverse_rms(values):
    return lax.rsqrt(jnp.mean(values * values, axis=-1, keepdims=True) + epsilon)


def dot_nn(a, b):
    return lax.dot_general(a, b, (((1,), (0,)), ((), ())), preferred_element_type=f32)


def dot_nt(a, b):
    return lax.dot_general(a, b, (((1,), (1,)), ((), ())), preferred_element_type=f32)


def dot_tn(a, b):
    return lax.dot_general(a, b, (((0,), (0,)), ((), ())), preferred_element_type=f32)


def swap_halves(values):
    half = values.shape[-1] // 2
    return jnp.concatenate([values[:, half:], values[:, :half]], axis=-1)


def rope_tables(positions, head_width):
    half_width = head_width // 2
    freq_index = jnp.arange(half_width).astype(f32)
    frequency = rope_base ** (-(2.0 * freq_index) / head_width)
    angles = positions.astype(f32)[..., None] * frequency
    cosine, sine = jnp.cos(angles), jnp.sin(angles)
    return (
        jnp.concatenate([cosine, cosine], axis=-1),
        jnp.concatenate([-sine, sine], axis=-1),
    )


def attention_forward_kernel(
    core_ref,
    own_ref,
    other_ref,
    cos_ref,
    sin_ref,
    seg_col_ref,
    seg_row_ref,
    gain_ref,
    o_own_ref,
    o_other_ref,
    p_ref,
    qkv_ref,
    o_ref,
):
    length = cos_ref.shape[1]
    half = length // 2
    own_rows = pl.ds(pl.multiple_of(core_ref[0] * half, half), half)
    other_rows = pl.ds(pl.multiple_of((1 - core_ref[0]) * half, half), half)

    def forward_one(seq):
        qkv_ref[seq, own_rows, :] = own_ref[seq]
        qkv_ref[seq, other_rows, :] = other_ref[seq]
        qkv = qkv_ref[seq]
        cosine, sine = cos_ref[seq], sin_ref[seq]
        row = lax.broadcasted_iota(jnp.int32, (length, length), 0)
        col = lax.broadcasted_iota(jnp.int32, (length, length), 1)
        allowed = (col <= row) & (seg_col_ref[seq] == seg_row_ref[seq])

        def rotated(lo, gain):
            raw = qkv[:, lo : lo + HD]
            normed = raw * inverse_rms(raw) * gain
            return (normed * cosine + swap_halves(normed) * sine).astype(bf16)

        key = rotated(2 * HD, gain_ref[1:2, :])
        value = qkv[:, 3 * HD : 4 * HD].astype(bf16)
        outs = []
        for head in range(2):
            query = rotated(head * HD, gain_ref[0:1, :])
            scores = jnp.where(allowed, dot_nt(query, key) * HD**-0.5, masked_score)
            row_max = jnp.max(scores, axis=-1, keepdims=True)
            raised = jnp.exp(scores - row_max)
            total = jnp.sum(raised, axis=-1, keepdims=True)
            weights = (raised * (1.0 / total)).astype(bf16)
            p_ref[seq, head] = weights
            outs.append(dot_nn(weights, value))
        o_ref[seq] = jnp.concatenate(outs, axis=-1)
        o_own_ref[seq] = o_ref[seq, own_rows, :].astype(bf16)
        o_other_ref[seq] = o_ref[seq, other_rows, :].astype(bf16)

    for seq in range(cos_ref.shape[0]):
        forward_one(seq)


def attention_backward_kernel(
    core_ref,
    own_ref,
    other_ref,
    do_own_ref,
    do_other_ref,
    cos_ref,
    sin_ref,
    gain_ref,
    p_ref,
    d_own_ref,
    d_other_ref,
    dgain_ref,
    qkv_ref,
    do_ref,
):
    length = cos_ref.shape[1]
    half = length // 2
    own_rows = pl.ds(pl.multiple_of(core_ref[0] * half, half), half)
    other_rows = pl.ds(pl.multiple_of((1 - core_ref[0]) * half, half), half)

    def backward_one(seq):
        qkv_ref[seq, own_rows, :] = own_ref[seq]
        qkv_ref[seq, other_rows, :] = other_ref[seq]
        do_ref[seq, own_rows, :] = do_own_ref[seq].astype(f32)
        do_ref[seq, other_rows, :] = do_other_ref[seq].astype(f32)
        qkv = qkv_ref[seq]
        cosine, sine = cos_ref[seq], sin_ref[seq]
        grad_o = do_ref[seq].astype(bf16)

        def forward(lo, gain):
            raw = qkv[:, lo : lo + HD]
            scale = inverse_rms(raw)
            unit = raw * scale
            normed = unit * gain
            return unit, scale, (normed * cosine + swap_halves(normed) * sine).astype(bf16)

        def backward(grad_rot, unit, scale, gain):
            grad_normed = grad_rot * cosine - swap_halves(grad_rot) * sine
            gain_part = jnp.sum(unit * grad_normed, axis=0, keepdims=True)
            weighted = grad_normed * gain
            mean = jnp.mean(weighted * unit, axis=-1, keepdims=True)
            return scale * (weighted - unit * mean), gain_part

        query_gain, key_gain = gain_ref[0:1, :], gain_ref[1:2, :]
        key_unit, key_scale, key = forward(2 * HD, key_gain)
        value = qkv[:, 3 * HD : 4 * HD].astype(bf16)
        grad_key = jnp.zeros((length, HD), f32)
        grad_value = jnp.zeros((length, HD), f32)
        query_gain_part = jnp.zeros((1, HD), f32)
        parts = []
        for head in range(2):
            query_unit, query_scale, query = forward(head * HD, query_gain)
            low = p_ref[seq, head]
            wide = low.astype(f32)
            grad_head = grad_o[:, head * HD : (head + 1) * HD]
            grad_weights = dot_nt(grad_head, value)
            delta = jnp.sum(wide * grad_weights, axis=-1, keepdims=True)
            grad_scores = (wide * (grad_weights - delta) * HD**-0.5).astype(bf16)
            grad_value += dot_tn(low, grad_head)
            grad_key += dot_tn(grad_scores, query)
            part, gain_part = backward(dot_nn(grad_scores, key), query_unit, query_scale, query_gain)
            query_gain_part += gain_part
            parts.append(part)
        part, key_gain_part = backward(grad_key, key_unit, key_scale, key_gain)
        parts += [part, grad_value]
        qkv_ref[seq] = jnp.concatenate(parts, axis=-1)
        d_own_ref[seq] = qkv_ref[seq, own_rows, :].astype(bf16)
        d_other_ref[seq] = qkv_ref[seq, other_rows, :].astype(bf16)
        dgain_ref[seq] = jnp.concatenate([query_gain_part, key_gain_part], axis=-1)

    for seq in range(cos_ref.shape[0]):
        backward_one(seq)


def seq_block(*shape):
    return pl.BlockSpec((STEP,) + shape, lambda s, c: (s,) + (0,) * len(shape))


def attention_forward(core, own, other, cosine, sine, seg_col, seg_row, gains):
    seqs, half, width = own.shape
    length = 2 * half
    return pl.pallas_call(
        attention_forward_kernel,
        grid_spec=pltpu.PrefetchScalarGridSpec(
            num_scalar_prefetch=1,
            grid=(seqs // STEP,),
            in_specs=[
                seq_block(half, width),
                seq_block(half, width),
                seq_block(length, HD),
                seq_block(length, HD),
                seq_block(length, 1),
                seq_block(1, length),
                pl.BlockSpec((2, HD), lambda s, c: (0, 0)),
            ],
            out_specs=[
                seq_block(half, 2 * HD),
                seq_block(half, 2 * HD),
                seq_block(2, length, length),
            ],
            scratch_shapes=[
                pltpu.VMEM((STEP, length, width), f32),
                pltpu.VMEM((STEP, length, 2 * HD), f32),
            ],
        ),
        out_shape=[
            jax.ShapeDtypeStruct((seqs, half, 2 * HD), bf16),
            jax.ShapeDtypeStruct((seqs, half, 2 * HD), bf16),
            jax.ShapeDtypeStruct((seqs, 2, length, length), bf16),
        ],
        compiler_params=pltpu.CompilerParams(vmem_limit_bytes=48 << 20),
        cost_estimate=SMALL_COST,
        name="attention_forward",
    )(core, own, other, cosine, sine, seg_col, seg_row, gains)


def attention_backward(core, own, other, do_own, do_other, cosine, sine, gains, weights):
    seqs, half, width = own.shape
    length = 2 * half
    return pl.pallas_call(
        attention_backward_kernel,
        grid_spec=pltpu.PrefetchScalarGridSpec(
            num_scalar_prefetch=1,
            grid=(seqs // STEP,),
            in_specs=[
                seq_block(half, width),
                seq_block(half, width),
                seq_block(half, 2 * HD),
                seq_block(half, 2 * HD),
                seq_block(length, HD),
                seq_block(length, HD),
                pl.BlockSpec((2, HD), lambda s, c: (0, 0)),
                seq_block(2, length, length),
            ],
            out_specs=[
                seq_block(half, width),
                seq_block(half, width),
                seq_block(1, 2 * HD),
            ],
            scratch_shapes=[
                pltpu.VMEM((STEP, length, width), f32),
                pltpu.VMEM((STEP, length, 2 * HD), f32),
            ],
        ),
        out_shape=[
            jax.ShapeDtypeStruct((seqs, half, width), bf16),
            jax.ShapeDtypeStruct((seqs, half, width), bf16),
            jax.ShapeDtypeStruct((seqs, 1, 2 * HD), f32),
        ],
        compiler_params=pltpu.CompilerParams(vmem_limit_bytes=48 << 20),
        cost_estimate=SMALL_COST,
        name="attention_backward",
    )(core, own, other, do_own, do_other, cosine, sine, gains, weights)


def ffn_kernel(n_ref, g_ref, w_ref, dn_ref, y_ref, z_ref, d_ref):
    units = z_ref.shape[1]
    gate_up = dot_nn(n_ref[...], w_ref[:, : 2 * units])
    grad_act = dot_nn(g_ref[...], w_ref[:, 2 * units :])
    gate, up = gate_up[:, :units], gate_up[:, units:]
    sigmoid = 1.0 / (1.0 + jnp.exp(-gate))
    silu = gate * sigmoid
    activated = (silu * up).astype(bf16)
    grad_gate = grad_act * up * sigmoid * (1.0 + gate * (1.0 - sigmoid))
    grad = jnp.concatenate([grad_gate, grad_act * silu], axis=-1).astype(bf16)
    d_ref[...] = grad
    z_ref[...] = activated
    dn_ref[...] = dot_nt(grad, w_ref[:, : 2 * units]).astype(dn_ref.dtype)
    y_ref[...] = dot_nt(activated, w_ref[:, 2 * units :]).astype(y_ref.dtype)


def ffn_half(normed, grads, weights, kind):
    tokens, width = normed.shape
    columns = weights.shape[1]
    units = columns // 3
    tile = tokens // 2

    def rows_of(n):
        return pl.BlockSpec((tile, n), lambda i: (i, 0))

    return pl.pallas_call(
        ffn_kernel,
        grid=(tokens // tile,),
        in_specs=[
            rows_of(width),
            rows_of(width),
            pl.BlockSpec((width, columns), lambda i: (0, 0)),
        ],
        out_specs=[rows_of(width)] * 2 + [rows_of(units), rows_of(2 * units)],
        out_shape=[jax.ShapeDtypeStruct((tokens, width), kind)] * 2
        + [
            jax.ShapeDtypeStruct((tokens, units), bf16),
            jax.ShapeDtypeStruct((tokens, 2 * units), bf16),
        ],
        compiler_params=pltpu.CompilerParams(vmem_limit_bytes=48 << 20),
        cost_estimate=SMALL_COST,
        name="ffn_half",
    )(normed, grads, weights)


def ffn_grads_kernel(n0_ref, n1_ref, g0_ref, g1_ref, d0_ref, d1_ref, z0_ref, z1_ref, out_ref):
    pair = d0_ref.shape[1]

    def product(x0, x1, y0, y1):
        return (dot_tn(x0[...], y0[...]) + dot_tn(x1[...], y1[...])).astype(bf16)

    out_ref[:, :pair] = product(n0_ref, n1_ref, d0_ref, d1_ref)
    out_ref[:, pair:] = product(g0_ref, g1_ref, z0_ref, z1_ref)


def ffn_grads_call(normed, grads, grad_pairs, activated):
    tokens, width = normed[0].shape
    units = activated[0].shape[1]
    tile = width // 4
    slab = pl.BlockSpec((tokens, tile), lambda i: (0, i))

    def whole(n):
        return pl.BlockSpec((tokens, n), lambda i: (0, 0))

    return pl.pallas_call(
        ffn_grads_kernel,
        grid=(width // tile,),
        in_specs=[slab] * 4 + [whole(2 * units)] * 2 + [whole(units)] * 2,
        out_specs=pl.BlockSpec((tile, 3 * units), lambda i: (i, 0)),
        out_shape=jax.ShapeDtypeStruct((width, 3 * units), bf16),
        compiler_params=pltpu.CompilerParams(vmem_limit_bytes=48 << 20),
        cost_estimate=pl.CostEstimate(
            flops=4 * tokens * width * 3 * units,
            transcendentals=0,
            bytes_accessed=4 * tokens * (2 * width + 3 * units) + 6 * width * units,
        ),
        name="ffn_grads",
    )(*normed, *grads, *grad_pairs, *activated)


def unxor(blocks, index):
    step = 1
    while step < len(blocks):
        odd = (index & step) != 0
        blocks = [
            jnp.where(odd, blocks[k ^ step], blocks[k]) for k in range(len(blocks))
        ]
        step *= 2
    return blocks


def pick(stacked, index):
    return lax.dynamic_index_in_dim(stacked, index, 0, keepdims=False)


def after(value, *others):
    return lax.optimization_barrier((value,) + others)[0]


def solution(mesh):
    devices = mesh.shape["dp"]
    depth = devices // PLANE
    lines = [[place + PLANE * k for k in range(depth)] for place in range(PLANE)]

    def dp_swap(value, mask):
        return lax.ppermute(value, "dp", [(i, i ^ mask) for i in range(devices)])

    def core_swap(value):
        return lax.ppermute(value, "tensor", [(0, 1), (1, 0)])

    def body(
        block_input,
        segments,
        positions,
        norm1_gain,
        w_query,
        w_key,
        w_value,
        w_out,
        query_gain,
        key_gain,
        norm2_gain,
        w_gate,
        w_up,
        w_down,
        grad_out,
    ):
        me = lax.axis_index("dp")
        core = lax.axis_index("tensor")
        place, level = me % PLANE, me // PLANE
        half, width = block_input.shape
        length = 2 * half
        rows = w_query.shape[0]
        band = PLANE * rows
        units = w_gate.shape[1] // PLANE

        def quarters(*arrays):
            parts = [jnp.moveaxis(a.reshape(rows, PLANE, -1), 1, 0) for a in arrays]
            return jnp.concatenate(parts, axis=-1)

        def plane_exchange(stacked, *marks):
            received = [pick(stacked, place)]
            for k in range(1, PLANE):
                received.append(after(dp_swap(pick(stacked, place ^ k), k), *marks))
            return jnp.stack(unxor(received, place))

        def gather_chips(block, *marks):
            chips = [block] + [after(dp_swap(block, k), *marks) for k in range(1, PLANE)]
            return jnp.concatenate(chips, axis=0)

        def reduce_chips(mine, *marks):
            mine = mine.reshape(PLANE, half, width)
            total = mine[0]
            for k in range(1, PLANE):
                total += after(dp_swap(mine[k].astype(bf16), k), *marks).astype(f32)
            return total

        gain_one = norm1_gain.astype(f32)
        gain_two = norm2_gain.astype(f32)
        head_gains = jnp.stack([query_gain, key_gain]).astype(f32)
        core_index = core.astype(jnp.int32).reshape(1)

        attn_stack = quarters(w_query, w_key, w_value, w_out.T)
        attn_width = attn_stack.shape[-1]
        layout = jnp.concatenate([segments[0], positions[0] // 256, positions[0] % 256])
        layout_rows = -(-layout.shape[0] // attn_width)
        layout = jnp.pad(layout, (0, layout_rows * attn_width - layout.shape[0]))
        layout = layout.astype(bf16).reshape(layout_rows, attn_width)
        layout_all = jnp.broadcast_to(layout, (PLANE,) + layout.shape)
        attn_stack = jnp.concatenate([attn_stack, layout_all], axis=1)
        received = [pick(attn_stack, place)]
        for k in range(1, PLANE):
            received.append(dp_swap(pick(attn_stack, place ^ k), k))
        layouts = jnp.stack([r[rows:] for r in received]).reshape(PLANE, -1)
        layouts = layouts[:, : 3 * length].astype(f32).reshape(PLANE, 3, length)
        attn_band = jnp.concatenate(unxor([r[:rows] for r in received], place), axis=0)
        ffn_stack = after(quarters(w_gate, w_up, w_down.T), attn_stack)
        ffn_stack = with_layout_constraint(ffn_stack, Layout(major_to_minor=(0, 1, 2)))
        ffn_band = plane_exchange(ffn_stack).reshape(band, 3 * units)
        ffn_band = with_layout_constraint(ffn_band, Layout(major_to_minor=(0, 1)))
        ffn_weights = lax.all_gather(ffn_band, "dp", axis_index_groups=lines)
        ffn_weights = with_layout_constraint(ffn_weights, Layout(major_to_minor=(0, 1, 2)))
        ffn_weights = ffn_weights.reshape(width, 3 * units)

        bands = [attn_band]
        for k in range(1, depth):
            bands.append(dp_swap(attn_band, k * PLANE))
        attn_weights = jnp.concatenate(unxor(bands, level), axis=0)
        own_x = gather_chips(after(block_input, ffn_band, bands[1]))
        other_x = core_swap(own_x)

        w_qkv, w_out_t = attn_weights[:, : 4 * HD], attn_weights[:, 4 * HD :]

        def units_of(block):
            wide = block.astype(f32)
            return wide * inverse_rms(wide)

        x_pair = (own_x, other_x)
        n1_pair = [(units_of(x) * gain_one).astype(bf16) for x in x_pair]
        qkv_pair = [dot_nn(n, w_qkv).reshape(PLANE, half, 4 * HD) for n in n1_pair]
        layouts = after(layouts, ffn_band)
        cosine, sine = rope_tables(layouts[:, 1] * 256.0 + layouts[:, 2], HD)
        seg_row, seg_col = layouts[:, 0:1], layouts[:, 0, :, None]
        o_own, o_other, weights = attention_forward(
            core_index, *qkv_pair, cosine, sine, seg_col, seg_row, head_gains
        )
        o_own, o_other = o_own.reshape(-1, 2 * HD), o_other.reshape(-1, 2 * HD)
        own_go = gather_chips(after(grad_out, attn_weights, own_x), o_own)
        o_other = after(o_other, own_go)
        other_go = core_swap(own_go)

        own_input = block_input.astype(f32)
        scale_one = inverse_rms(own_input)
        unit_one = own_input * scale_one
        sent = core_swap(dot_nt(o_other, w_out_t).astype(bf16))
        hidden = own_input + reduce_chips(dot_nt(o_own, w_out_t) + sent.astype(f32))
        scale_two = inverse_rms(hidden)
        unit_two = hidden * scale_two
        normed_two = (unit_two * gain_two).astype(bf16)
        own_n2 = gather_chips(normed_two)
        other_n2 = core_swap(own_n2)

        dn_other, y_other, z_other, d_other = ffn_half(
            other_n2, other_go, ffn_weights, bf16
        )
        sent = core_swap(dn_other)
        dn_own, y_own, z_own, d_own = ffn_half(after(own_n2, dn_other), own_go, ffn_weights, f32)
        dn_sum = dn_own + sent.astype(f32)
        grad_normed_two = reduce_chips(dn_sum)

        ffn_partial = ffn_grads_call(
            (own_n2, other_n2),
            (own_go, other_go),
            (d_own, d_other),
            (z_own, z_other),
        )
        ffn_total = lax.psum_scatter(
            ffn_partial.reshape(depth, band, 3 * units), "dp", axis_index_groups=lines
        )

        gain_two_part = jnp.sum(unit_two * grad_normed_two, axis=0)
        weighted_two = grad_normed_two * gain_two
        grad_hidden = grad_out.astype(f32) + scale_two * (
            weighted_two - unit_two * jnp.mean(weighted_two * unit_two, axis=-1, keepdims=True)
        )
        grad_hidden = after(grad_hidden, ffn_partial)
        own_dh = gather_chips(grad_hidden.astype(bf16))
        other_dh = core_swap(own_dh)

        y_sum = after(y_own + core_swap(y_other).astype(f32), own_dh)
        do_pair = [
            dot_nn(dh, w_out_t).astype(bf16).reshape(PLANE, half, 2 * HD)
            for dh in (own_dh, other_dh)
        ]
        dqkv_own, dqkv_other, head_gain_parts = attention_backward(
            core_index, *qkv_pair, *do_pair, cosine, sine, head_gains, weights
        )
        block_out = (hidden + reduce_chips(y_sum, dqkv_own)).astype(bf16)
        dqkv_own = after(dqkv_own, block_out).reshape(-1, 4 * HD)
        dqkv_other = dqkv_other.reshape(-1, 4 * HD)

        ffn_total = after(ffn_total, dqkv_own)
        sent = core_swap(dot_nt(dqkv_other, w_qkv).astype(bf16))
        dn1_own = dot_nt(dqkv_own, w_qkv)
        dn1_sum = dn1_own + sent.astype(f32)
        attn_partial = jnp.concatenate(
            [
                dot_tn(n1_pair[0], dqkv_own) + dot_tn(n1_pair[1], dqkv_other),
                dot_tn(own_dh, o_own) + dot_tn(other_dh, o_other),
            ],
            axis=-1,
        ).astype(bf16).reshape(depth, band, attn_width)

        gain_one_part = jnp.sum(units_of(own_x) * dn1_sum, axis=0)
        gain_parts = jnp.concatenate(
            [gain_one_part, gain_two_part, jnp.sum(head_gain_parts, axis=(0, 1))]
        )
        gain_count = gain_parts.shape[0]
        gain_rows = -(-gain_count // attn_width)

        def two_parts(sums):
            high = sums.astype(bf16)
            return jnp.concatenate([high, (sums - high.astype(f32)).astype(bf16)], axis=0)

        def joined(extra):
            extra = extra.astype(f32)
            return extra[:gain_rows] + extra[gain_rows:]

        gain_sum = jnp.pad(gain_parts, (0, gain_rows * attn_width - gain_count))
        gain_sum = gain_sum.reshape(gain_rows, attn_width)
        extra = two_parts(gain_sum)
        total = pick(attn_partial, level).astype(f32)
        messages = []
        for k in range(1, depth):
            message = jnp.concatenate([pick(attn_partial, level ^ k), extra], axis=0)
            message = dp_swap(after(message, ffn_total), k * PLANE)
            messages.append(message)
            total += message[:band].astype(f32)
            gain_sum += joined(message[band:])
        ffn_grads = plane_exchange(ffn_total.reshape(PLANE, rows, 3 * units), *messages)
        ffn_grads = jnp.moveaxis(ffn_grads, 0, 1).astype(f32)


        grad_normed_one = reduce_chips(dn1_sum, messages[-1])
        total = total.astype(bf16).reshape(PLANE, rows, attn_width)
        extra = two_parts(gain_sum)
        received = [pick(total, place)]
        for k in range(1, PLANE):
            message = jnp.concatenate([pick(total, place ^ k), extra], axis=0)
            message = dp_swap(message, k)
            received.append(message[:rows])
            gain_sum += joined(message[rows:])
        attn_grads = jnp.stack(unxor(received, place), axis=1).astype(f32)
        gain_sum = (gain_sum + core_swap(gain_sum)).reshape(-1)

        weighted_one = grad_normed_one * gain_one
        grad_input = grad_hidden + scale_one * (
            weighted_one - unit_one * jnp.mean(weighted_one * unit_one, axis=-1, keepdims=True)
        )

        def columns(grads, lo, hi):
            return grads[:, :, lo:hi].reshape(rows, -1)

        return (
            block_out,
            grad_input,
            gain_sum[:width],
            columns(attn_grads, 0, 2 * HD),
            columns(attn_grads, 2 * HD, 3 * HD),
            columns(attn_grads, 3 * HD, 4 * HD),
            columns(attn_grads, 4 * HD, 6 * HD).T,
            gain_sum[2 * width : 2 * width + HD],
            gain_sum[2 * width + HD : 2 * width + 2 * HD],
            gain_sum[width : 2 * width],
            columns(ffn_grads, 0, units),
            columns(ffn_grads, units, 2 * units),
            columns(ffn_grads, 2 * units, 3 * units).T,
        )

    in_specs = (
        P(("dp", "tensor"), None),
        P("dp", None),
        P("dp", None),
        P(),
        P("dp", "tensor"),
        P("dp", "tensor"),
        P("dp", "tensor"),
        P("tensor", "dp"),
        P(),
        P(),
        P(),
        P("dp", "tensor"),
        P("dp", "tensor"),
        P("tensor", "dp"),
        P(("dp", "tensor"), None),
    )
    out_specs = (
        P(("dp", "tensor"), None),
        P(("dp", "tensor"), None),
        P(),
        P("dp", "tensor"),
        P("dp", "tensor"),
        P("dp", "tensor"),
        P("tensor", "dp"),
        P(),
        P(),
        P(),
        P("dp", "tensor"),
        P("dp", "tensor"),
        P("tensor", "dp"),
    )
    return jax.shard_map(body, mesh=mesh, in_specs=in_specs, out_specs=out_specs, check_vma=False)
```
